32 devices in a mesh: gx: 8 (over z, x), gy: 4 (over y, core).
Axes of the slice: x: 2, y: 2, z: 4, core: 2. Of those that a mesh axis runs over, the one named last changes fastest.
Arguments:
- control: float32 [75, 128, 1024], P(None, 'gy', 'gx'), may hold values from -6 to 6
- east_coeff: float32 [75, 128, 1024], P(None, 'gy', 'gx'), may hold values from 0.12 to 0.245
- north_coeff: float32 [75, 128, 1024], P(None, 'gy', 'gx'), may hold values from 0.12 to 0.245
- ocean_mask: int32 [75, 128, 1024], P(None, 'gy', 'gx'), may hold values 0 or 1
- corner_cells: int32 [4, 131072], P(None, ('gx', 'gy')), may hold values from 0 to 4095, as said below
- corner_weights: float32 [4, 131072], P(None, ('gx', 'gy')), may hold values from 0 to 1, as said below
- obs_value: float32 [75, 131072], P(None, ('gx', 'gy')), may hold values from -6 to 6
- obs_precision: float32 [75, 131072], P(None, ('gx', 'gy')), may hold values from 0.3 to 3
- slot_counts: int32 [32, 32], P(('gx', 'gy')), may hold values from 1 to 128, as said below
Outputs:
- gradient: float32 [75, 128, 1024], P(None, 'gy', 'gx')
- departures: float32 [75, 131072], P(None, ('gx', 'gy'))
The draws below stay inside these ranges and needn't reach their ends.
Inputs may be any that keep to these rules, and one draw needn't show every extreme that they name: For each slot, corner_cells lists the cells (r, s), (r, s + 1), (r + 1, s), (r + 1, s + 1) of one grid cell with r < 31 and s < 127, numbered r * 128 + s in the holding device's tile, in that order. `corner_weights`: the four weights of a slot are the bilinear weights (1 - a)(1 - b), a(1 - b), (1 - a)b, ab of two fractions a, b in [0, 1]; they sum to 1. slot_counts[d, p] counts the live slots that device p holds for owner d; for every owner some device sends exactly 128 live slots.
All inputs are finite; a program needn't handle non-finite values. No bound on the sum of `ocean_mask` on one device may be relied on, other than what follows from the above.
Results may differ from the reference program's by a relative error of at most 0.00002.
Values sent between devices are 32-bit elements; how exact they have to be, the bound alone decides.
No kernel may reach another device: no remote copies, remote signals or barrier semaphores. Data moves between devices by JAX's collectives and lax.ppermute only.
A program may use at most 128 MiB of HBM per device.

```python
import math
import jax
import jax.numpy as jnp

CX = 128
CY = 32
LEV = 75
STEPS = 4
SLOTS_DEV = 4096
CAP = 128
NLAT = 128
NLON = 1024
N_GX = 8
N_GY = 4
DEVICES = 32


def draw_slot_counts(key, part):
    key_level, key_base, key_full = jax.random.split(jax.random.fold_in(key, 17), 3)
    density = jax.random.randint(key_level, (DEVICES, 1), 1, 4)
    base = jax.random.randint(key_base, (DEVICES, DEVICES), 1, CAP + 1)
    counts = jnp.minimum(CAP, base * density // 3 + 1)
    chosen = jax.random.permutation(key_full, DEVICES)
    full = jnp.arange(DEVICES)[None, :] == chosen[:, None]
    return jnp.where(full, CAP, counts).astype(jnp.int32)


def draw_corner_cells(key, part):
    key_row, key_col = jax.random.split(jax.random.fold_in(key, 29), 2)
    total = DEVICES * SLOTS_DEV
    row_start = jax.random.randint(key_row, (total,), 0, CY - 1)
    col_start = jax.random.randint(key_col, (total,), 0, CX - 1)
    anchor = row_start * CX + col_start
    return jnp.stack([anchor, anchor + 1, anchor + CX, anchor + CX + 1]).astype(jnp.int32)


def draw_corner_weights(key, part):
    key_east, key_north = jax.random.split(jax.random.fold_in(key, 31), 2)
    total = DEVICES * SLOTS_DEV
    frac_east = jax.random.uniform(key_east, (total,), jnp.float32, 0.0, 1.0)
    frac_north = jax.random.uniform(key_north, (total,), jnp.float32, 0.0, 1.0)
    return jnp.stack([(1.0 - frac_east) * (1.0 - frac_north), frac_east * (1.0 - frac_north), (1.0 - frac_east) * frac_north, frac_east * frac_north]).astype(jnp.float32)


def plant(values, stream_key, least, top_value):
    longest = values.shape.index(max(values.shape))
    spots = []
    for shift in (0, 1):
        where = [jax.random.randint(jax.random.fold_in(stream_key, axis), (), 0, length) for axis, length in enumerate(values.shape)]
        where[longest] = (where[longest] + shift) % values.shape[longest]
        spots.append(tuple(where))
    return values.at[spots[0]].set(least).at[spots[1]].set(top_value)


def shard_levels(own_key, shape, cuts, smallest, high):
    factor_of, own = 1.0, jax.random.fold_in(own_key, 6)
    for dim, blocks in cuts:
        steps = jnp.exp(jax.random.uniform(jax.random.fold_in(own, dim), (blocks,), jnp.float32, smallest / len(cuts), high / len(cuts)))
        factor_of = factor_of * jnp.repeat(steps, shape[dim] // blocks).reshape([-1 if axis == dim else 1 for axis in range(len(shape))])
    return factor_of


def normal_values(rng, dims, scale, limit, pieces=(), held_as=jnp.bfloat16):
    drawn = scale * jax.random.normal(rng, dims, jnp.float32)
    if pieces:
        drawn = drawn * shard_levels(rng, dims, pieces, -0.22, 0.18)
    return jnp.clip(drawn, -limit, limit).astype(held_as)


def setup_inputs(seed: int = 0) -> dict:
    splits = jax.random.split(jax.random.key(seed), 10)
    control = normal_values(splits[0], (LEV, NLAT, NLON), 1.0, 6.0, ((1, 4), (2, 8)), jnp.float32)
    east_coeff = jnp.clip(0.12 + 0.125 * jax.random.uniform(splits[1], (LEV, NLAT, NLON), jnp.float32) ** shard_levels(splits[1], (LEV, NLAT, NLON), ((1, 4), (2, 8)), -0.2, 0.2), 0.12, 0.245)
    north_coeff = jnp.clip(0.12 + 0.125 * jax.random.uniform(splits[2], (LEV, NLAT, NLON), jnp.float32) ** shard_levels(splits[2], (LEV, NLAT, NLON), ((1, 4), (2, 8)), -0.2, 0.2), 0.12, 0.245)
    ocean_mask = plant((jax.random.randint(splits[3], (LEV, NLAT, NLON), 0, 5) < 4).astype(jnp.int32), jax.random.fold_in(splits[3], 1), 0, 1)
    corner_cells = draw_corner_cells(jax.random.fold_in(splits[9], 71), 0)
    corner_weights = draw_corner_weights(jax.random.fold_in(splits[9], 71), 0)
    obs_value = normal_values(splits[6], (LEV, DEVICES * SLOTS_DEV), 1.0, 6.0, ((1, 32),), jnp.float32)
    obs_precision = jnp.clip(jnp.exp(math.log(3.0) - 2.3025851 * jax.random.uniform(splits[7], (LEV, DEVICES * SLOTS_DEV), jnp.float32) ** shard_levels(splits[7], (LEV, DEVICES * SLOTS_DEV), ((1, 32),), -0.2, 0.2)), 0.3, 3.0)
    slot_counts = draw_slot_counts(jax.random.fold_in(splits[9], 71), 0)
    return {"control": control, "east_coeff": east_coeff, "north_coeff": north_coeff, "ocean_mask": ocean_mask, "corner_cells": corner_cells, "corner_weights": corner_weights, "obs_value": obs_value, "obs_precision": obs_precision, "slot_counts": slot_counts}


def reference(control, east_coeff, north_coeff, ocean_mask, corner_cells, corner_weights, obs_value, obs_precision, slot_counts):
    lat_cells = CY * N_GY
    lon_cells = CX * N_GX
    devices_all = N_GX * N_GY
    capacity = SLOTS_DEV // devices_all
    masked = ocean_mask.astype(jnp.float32)
    east = east_coeff * masked * jnp.roll(masked, -1, 2)
    row_keep = (jnp.arange(lat_cells) < lat_cells - 1).astype(jnp.float32)
    north = north_coeff * masked * jnp.roll(masked, -1, 1) * row_keep[None, :, None]
    east_west = jnp.roll(east, 1, 2)
    north_south = jnp.roll(north, 1, 1)

    def sweep(values):
        return (values + east * (jnp.roll(values, -1, 2) - values)
                - east_west * (values - jnp.roll(values, 1, 2))
                + north * (jnp.roll(values, -1, 1) - values)
                - north_south * (values - jnp.roll(values, 1, 1)))

    def diffuse(values):
        for sweep_count in range(STEPS):
            values = sweep(values)
        return values

    background = diffuse(masked * control)
    column = jnp.arange(devices_all * SLOTS_DEV, dtype=jnp.int32)
    source = column // SLOTS_DEV
    lon_block = source // N_GY
    lat_block = source % N_GY
    latitude = lat_block[None, :] * CY + corner_cells // CX
    longitude = lon_block[None, :] * CX + corner_cells % CX
    global_cell = (latitude * lon_cells + longitude).astype(jnp.int32)
    flat = background.reshape(LEV, -1)
    equivalent = jnp.zeros((LEV, devices_all * SLOTS_DEV), jnp.float32)
    for corner in range(4):
        equivalent = equivalent + corner_weights[corner][None, :] * jnp.take(flat, global_cell[corner], axis=1)

    def reorder(values):
        return values.reshape(LEV, devices_all, devices_all, capacity).transpose(0, 2, 1, 3).reshape(LEV, -1)

    received = reorder(equivalent)
    live = (slot_counts[:, :, None] > jnp.arange(capacity)[None, None, :]).reshape(-1)
    departures = jnp.where(live[None, :], obs_precision * (received - obs_value), jnp.float32(0.0))
    back = reorder(departures)
    adjoint = jnp.zeros((LEV, lat_cells * lon_cells), jnp.float32)
    for corner in range(4):
        adjoint = adjoint.at[:, global_cell[corner]].add(corner_weights[corner][None, :] * back)
    gradient = masked * (control + diffuse(adjoint.reshape(LEV, lat_cells, lon_cells)))
    return gradient, departures
```

```python
import functools

import jax
import jax.numpy as jnp
from jax import lax
from jax.experimental import pallas as pl
from jax.experimental.pallas import tpu as pltpu
from jax.sharding import PartitionSpec as P

F32, BF16 = jnp.float32, jnp.bfloat16
VMEM = pltpu.VMEM
def split2(x):
    hi = x.astype(BF16)
    lo = (x - hi.astype(F32)).astype(BF16)
    return hi, lo

def hats(cells_ref, weights_ref, j0, n, rows, cols):
    c = cells_ref[0:1, pl.ds(j0, n)]
    w = weights_ref[:, pl.ds(j0, n)]
    r = c // cols
    s = c - r * cols
    east, west = w[1:2] + w[3:4], w[0:1] + w[2:3]
    north, south = w[2:3] + w[3:4], w[0:1] + w[1:2]
    return r, s, east, west, north, south

def hat(index, low, high, size):
    at = lax.broadcasted_iota(jnp.int32, (size, index.shape[1]), 0) - index
    return jnp.where(at == 0, low, jnp.where(at == 1, high, 0.0))

def gather_kernel(rows, lev, cols, nb, cells_ref, weights_ref, bg_ref, out_ref, bb, t0, t1, rr0, rr1):
    for r in range(rows):
        hi, lo = split2(bg_ref[r])
        bb[r * lev:(r + 1) * lev, 0:cols] = hi
        bb[r * lev:(r + 1) * lev, cols:2 * cols] = lo
    blk = 256
    def multiply(jb, t, rr):
        r, s, east, west, north, south = hats(cells_ref, weights_ref, pl.multiple_of(jb * blk, blk), blk, rows, cols)
        rr[...] = hat(r, south, north, rows)
        hi, lo = split2(hat(s, west, east, cols))
        left = bb[...]
        t[...] = (jnp.dot(left, jnp.concatenate([hi, hi], 0), preferred_element_type=F32)
                  + jnp.dot(left, jnp.concatenate([lo, lo], 0), preferred_element_type=F32))
    def reduce(jb, t, rr):
        acc = jnp.zeros((lev, blk), F32)
        for r in range(rows):
            acc = acc + t[r * lev:(r + 1) * lev, :] * rr[r:r + 1, :]
        out_ref[2 * jb] = acc[:, 0:128]
        out_ref[2 * jb + 1] = acc[:, 128:256]
    def step(i, _):
        multiply(2 * i, t0, rr0)
        multiply(2 * i + 1, t1, rr1)
        reduce(2 * i, t0, rr0)
        reduce(2 * i + 1, t1, rr1)
        return 0
    lax.fori_loop(0, nb // 2, step, 0)

def gather(cells, weights, bg, slots):
    rows, lev, cols = bg.shape
    nb = slots // 256
    return pl.pallas_call(functools.partial(gather_kernel, rows, lev, cols, nb),
        out_shape=jax.ShapeDtypeStruct((2 * nb, lev, 128), F32),
        in_specs=[pl.BlockSpec(memory_space=VMEM)] * 3,
        out_specs=pl.BlockSpec(memory_space=VMEM),
        scratch_shapes=[VMEM((rows * lev, 2 * cols), BF16), VMEM((rows * lev, 256), F32), VMEM((rows * lev, 256), F32), VMEM((rows, 256), F32), VMEM((rows, 256), F32)],
        compiler_params=pltpu.CompilerParams(vmem_limit_bytes=60 * 2**20),
    )(cells, weights, bg)

def scatter_kernel(rows, lev, cols, nb, cells_ref, weights_ref, back_ref, out_ref, x, acc):
    blk = 256
    acc[...] = jnp.zeros_like(acc)
    def step(jb, _):
        r, s, east, west, north, south = hats(cells_ref, weights_ref, pl.multiple_of(jb * blk, blk), blk, rows, cols)
        hi, lo = split2(hat(s, west, east, cols))
        right = jnp.concatenate([hi, lo], 0)
        back = jnp.concatenate([back_ref[2 * jb], back_ref[2 * jb + 1]], 1)
        u_hi, u_lo = split2(back * south)
        v_hi, v_lo = split2(back * north)
        one = hat(r, 1.0, 0.0, rows + 1).astype(BF16)
        for q in range(rows):
            at = jnp.broadcast_to(one[q:q + 1, :], (lev, blk))
            if q:
                below = jnp.broadcast_to(one[q - 1:q, :], (lev, blk))
                x[q * lev:(q + 1) * lev, 0:blk] = u_hi * at + v_hi * below
                x[q * lev:(q + 1) * lev, blk:] = u_lo * at + v_lo * below
            else:
                x[0:lev, 0:blk] = u_hi * at
                x[0:lev, blk:] = u_lo * at
        acc[...] += lax.dot_general(x[...], jnp.concatenate([right, right], 1), (((1,), (1,)), ((), ())), preferred_element_type=F32)
        return 0
    lax.fori_loop(0, nb, step, 0)
    for r in range(rows):
        a = acc[r * lev:(r + 1) * lev, :]
        out_ref[r] = a[:, 0:cols] + a[:, cols:]

def scatter(cells, weights, back, rows, cols):
    n2, lev, _ = back.shape
    nb = n2 // 2
    return pl.pallas_call(functools.partial(scatter_kernel, rows, lev, cols, nb),
        out_shape=jax.ShapeDtypeStruct((rows, lev, cols), F32),
        in_specs=[pl.BlockSpec(memory_space=VMEM)] * 3,
        out_specs=pl.BlockSpec(memory_space=VMEM),
        scratch_shapes=[VMEM((rows * lev, 512), BF16), VMEM((rows * lev, 256), F32)],
        compiler_params=pltpu.CompilerParams(vmem_limit_bytes=60 * 2**20),
    )(cells, weights, back)

STEPS = 4


def exchange(values, share):
    blocks, levels, width = values.shape
    if share > 1:
        values = values.reshape(blocks, levels, share, -1).transpose(0, 2, 1, 3)
    values = values.reshape(blocks * share, levels, width // share)
    values = lax.all_to_all(values, ("gx", "gy"), 0, 0, tiled=True)
    if share > 1:
        values = values.reshape(blocks, share, levels, -1).transpose(0, 2, 1, 3)
    return values.reshape(blocks, levels, width)


def with_halo(x, sides, width):
    for axis, dim in sides:
        size, length = (lax.axis_size(axis), x.shape[dim])
        up = [(i, (i + 1) % size) for i in range(size)]
        down = [(j, i) for i, j in up]
        last = lax.slice_in_dim(x, length - width, length, axis=dim)
        first = lax.slice_in_dim(x, 0, width, axis=dim)
        before = lax.ppermute(last, axis, up)
        after = lax.ppermute(first, axis, down)
        x = jnp.concatenate([before, x, after], axis=dim)
    return x


def sweep(padded, east, north):
    centre = padded[:, 1:-1, 1:-1]
    return (
        centre
        + east[:, 1:-1, 1:-1] * (padded[:, 1:-1, 2:] - centre)
        - east[:, 1:-1, :-2] * (centre - padded[:, 1:-1, :-2])
        + north[:, 1:-1, 1:-1] * (padded[:, 2:, 1:-1] - centre)
        - north[:, :-2, 1:-1] * (centre - padded[:, :-2, 1:-1])
    )


def body(
    control,
    east_coeff,
    north_coeff,
    ocean_mask,
    corner_cells,
    corner_weights,
    obs_value,
    obs_precision,
    slot_counts,
):
    levels, tile_rows, tile_cols = control.shape
    lat_index = lax.axis_index("gy")
    total_rows = tile_rows * lax.axis_size("gy")
    masked = ocean_mask.astype(jnp.float32)
    stacked = jnp.stack([masked, east_coeff, north_coeff])
    margin = STEPS
    rimmed = with_halo(stacked, (("gx", 3), ("gy", 2)), STEPS)
    mask_wide = rimmed[0]
    east = rimmed[1][:, :, :-1] * mask_wide[:, :, :-1] * mask_wide[:, :, 1:]
    east = jnp.pad(east, ((0, 0), (0, 0), (0, 1)))
    north = rimmed[2][:, :-1, :] * mask_wide[:, :-1, :] * mask_wide[:, 1:, :]
    global_rows = lat_index * tile_rows - margin + jnp.arange(tile_rows + 2 * margin - 1)
    row_keep = ((global_rows >= 0) & (global_rows < total_rows - 1)).astype(jnp.float32)
    north = jnp.pad(north * row_keep[None, :, None], ((0, 0), (0, 1), (0, 0)))

    def diffuse(current):
        padded = with_halo(current, (("gx", 2), ("gy", 1)), STEPS)
        for sweep_count in range(STEPS):
            remain = STEPS - sweep_count
            height = tile_rows + 2 * remain
            width_now = tile_cols + 2 * remain
            padded = sweep(
                padded,
                east[:, sweep_count : sweep_count + height, sweep_count : sweep_count + width_now],
                north[:, sweep_count : sweep_count + height, sweep_count : sweep_count + width_now],
            )
        return padded

    background = diffuse(masked * control)
    full = -(-levels // 16) * 16
    slots = corner_cells.shape[1]
    peers = lax.axis_size(("gx", "gy"))
    capacity = slots // peers
    share = 128 // capacity
    field = jnp.pad(background.transpose(1, 0, 2), ((0, 0), (0, full - levels), (0, 0)))
    equivalent = gather(corner_cells, corner_weights, field, slots)
    received = exchange(equivalent, share)
    counts = slot_counts[0].reshape(-1, share, 1)
    live = (counts > jnp.arange(capacity)).reshape(-1, 1, 128)
    received = received[:, :levels].transpose(1, 0, 2).reshape(levels, slots)
    departures = jnp.where(live.reshape(1, slots), obs_precision * (received - obs_value), jnp.float32(0.0))
    back = jnp.pad(departures.reshape(levels, -1, 128).transpose(1, 0, 2), ((0, 0), (0, full - levels), (0, 0)))
    adjoint = scatter(corner_cells, corner_weights, exchange(back, share), tile_rows, tile_cols)
    adjoint = adjoint[:, :levels].transpose(1, 0, 2)
    gradient = masked * (control + diffuse(adjoint))
    return (gradient, departures)


def solution(mesh):
    return jax.shard_map(
        body,
        mesh=mesh,
        in_specs=(
            P(None, "gy", "gx"),
            P(None, "gy", "gx"),
            P(None, "gy", "gx"),
            P(None, "gy", "gx"),
            P(None, ("gx", "gy")),
            P(None, ("gx", "gy")),
            P(None, ("gx", "gy")),
            P(None, ("gx", "gy")),
            P(("gx", "gy"), None),
        ),
        out_specs=(P(None, "gy", "gx"), P(None, ("gx", "gy"))),
        check_vma=False,
    )
```

```python
import functools

import jax
import jax.numpy as jnp
from jax import lax
from jax.experimental import pallas as pl
from jax.experimental.pallas import tpu as pltpu
from jax.sharding import PartitionSpec as P

F32, BF16 = jnp.float32, jnp.bfloat16
VMEM = pltpu.VMEM
STEPS = 4
LANES8 = 8
WHOLE = pl.BlockSpec(memory_space=pltpu.VMEM)


def split2(x):
    hi = x.astype(BF16)
    lo = (x - hi.astype(F32)).astype(BF16)
    return hi, lo

def hats(cells_ref, weights_ref, j0, n, rows, cols):
    c = cells_ref[0:1, pl.ds(j0, n)]
    w = weights_ref[:, pl.ds(j0, n)]
    r = c // cols
    s = c - r * cols
    east, west = w[1:2] + w[3:4], w[0:1] + w[2:3]
    north, south = w[2:3] + w[3:4], w[0:1] + w[1:2]
    return r, s, east, west, north, south

def hat(index, low, high, size):
    at = lax.broadcasted_iota(jnp.int32, (size, index.shape[1]), 0) - index
    return jnp.where(at == 0, low, jnp.where(at == 1, high, 0.0))

def gather_kernel(rows, lev, cols, nb, cells_ref, weights_ref, bg_ref, out_ref, bb, t0, t1, rr0, rr1):
    for r in range(rows):
        hi, lo = split2(bg_ref[r])
        bb[r * lev:(r + 1) * lev, 0:cols] = hi
        bb[r * lev:(r + 1) * lev, cols:2 * cols] = lo
    blk = 256
    def multiply(jb, t, rr):
        r, s, east, west, north, south = hats(cells_ref, weights_ref, pl.multiple_of(jb * blk, blk), blk, rows, cols)
        rr[...] = hat(r, south, north, rows)
        hi, lo = split2(hat(s, west, east, cols))
        left = bb[...]
        t[...] = (jnp.dot(left, jnp.concatenate([hi, hi], 0), preferred_element_type=F32)
                  + jnp.dot(left, jnp.concatenate([lo, lo], 0), preferred_element_type=F32))
    def reduce(jb, t, rr):
        acc = jnp.zeros((lev, blk), F32)
        for r in range(rows):
            acc = acc + t[r * lev:(r + 1) * lev, :] * rr[r:r + 1, :]
        out_ref[2 * jb] = acc[:, 0:128]
        out_ref[2 * jb + 1] = acc[:, 128:256]
    def step(i, _):
        multiply(2 * i, t0, rr0)
        multiply(2 * i + 1, t1, rr1)
        reduce(2 * i, t0, rr0)
        reduce(2 * i + 1, t1, rr1)
        return 0
    lax.fori_loop(0, nb // 2, step, 0)

def gather(cells, weights, bg, slots):
    rows, lev, cols = bg.shape
    nb = slots // 256
    return pl.pallas_call(functools.partial(gather_kernel, rows, lev, cols, nb),
        out_shape=jax.ShapeDtypeStruct((2 * nb, lev, 128), F32),
        in_specs=[pl.BlockSpec(memory_space=VMEM)] * 3,
        out_specs=pl.BlockSpec(memory_space=VMEM),
        scratch_shapes=[VMEM((rows * lev, 2 * cols), BF16), VMEM((rows * lev, 256), F32), VMEM((rows * lev, 256), F32), VMEM((rows, 256), F32), VMEM((rows, 256), F32)],
        compiler_params=params(20),
    )(cells, weights, bg)

def scatter_kernel(rows, lev, cols, nb, cells_ref, weights_ref, back_ref, out_ref, x, acc):
    blk = 256
    acc[...] = jnp.zeros_like(acc)
    def step(jb, _):
        r, s, east, west, north, south = hats(cells_ref, weights_ref, pl.multiple_of(jb * blk, blk), blk, rows, cols)
        hi, lo = split2(hat(s, west, east, cols))
        right = jnp.concatenate([hi, lo], 0)
        back = jnp.concatenate([back_ref[2 * jb], back_ref[2 * jb + 1]], 1)
        u_hi, u_lo = split2(back * south)
        v_hi, v_lo = split2(back * north)
        one = hat(r, 1.0, 0.0, rows + 1).astype(BF16)
        for q in range(rows):
            at = jnp.broadcast_to(one[q:q + 1, :], (lev, blk))
            if q:
                below = jnp.broadcast_to(one[q - 1:q, :], (lev, blk))
                x[q * lev:(q + 1) * lev, 0:blk] = u_hi * at + v_hi * below
                x[q * lev:(q + 1) * lev, blk:] = u_lo * at + v_lo * below
            else:
                x[0:lev, 0:blk] = u_hi * at
                x[0:lev, blk:] = u_lo * at
        acc[...] += lax.dot_general(x[...], jnp.concatenate([right, right], 1), (((1,), (1,)), ((), ())), preferred_element_type=F32)
        return 0
    lax.fori_loop(0, nb, step, 0)
    for r in range(rows):
        a = acc[r * lev:(r + 1) * lev, :]
        out_ref[r] = a[:, 0:cols] + a[:, cols:]

def scatter(cells, weights, back, rows, cols):
    n2, lev, _ = back.shape
    nb = n2 // 2
    return pl.pallas_call(functools.partial(scatter_kernel, rows, lev, cols, nb),
        out_shape=jax.ShapeDtypeStruct((rows, lev, cols), F32),
        in_specs=[pl.BlockSpec(memory_space=VMEM)] * 3,
        out_specs=pl.BlockSpec(memory_space=VMEM),
        scratch_shapes=[VMEM((rows * lev, 512), BF16), VMEM((rows * lev, 256), F32)],
        compiler_params=params(20),
    )(cells, weights, back)


def group_start(g, levels):
    start, last = LANES8 * g, levels - LANES8
    return min(start, last) if isinstance(g, int) else jnp.minimum(start, last)


def params(megabytes):
    return pltpu.CompilerParams(vmem_limit_bytes=megabytes * 2**20)


def lanes_of(g):
    return pl.ds(pl.multiple_of(LANES8 * g, LANES8), LANES8)


def stage_kernel(groups, levels, margin, control_ref, east_ref, north_ref, mask_ref, *outs):
    cols = control_ref.shape[2]
    refs = [ref.reshape(levels * LANES8, cols) for ref in (control_ref, east_ref, north_ref, mask_ref)]
    block, last = pl.program_id(0), pl.num_programs(0) - 1
    field_refs, top_ref, bottom_ref = outs[:4], outs[4], outs[5]
    def step(g, _):
        start = group_start(g, levels)
        for r in range(LANES8):
            where = pl.ds(start * LANES8 + r, LANES8, stride=LANES8)
            control, east, north, mask = (ref[where, :] for ref in refs)
            mask = mask.astype(F32)
            for ref, value in zip(field_refs, (mask * control, mask, east, north)):
                ref[r, lanes_of(g), :] = value
        return 0
    lax.fori_loop(0, groups, step, 0)
    @pl.when(block == 0)
    def _():
        for f in range(4):
            bottom_ref[f * margin:(f + 1) * margin] = field_refs[f][0:margin]
    @pl.when(block == last)
    def _():
        for f in range(4):
            top_ref[f * margin:(f + 1) * margin] = field_refs[f][LANES8 - margin:LANES8]


def stage(groups, margin, natural):
    levels, rows, cols = natural[0].shape
    depth = LANES8 * groups
    return pl.pallas_call(functools.partial(stage_kernel, groups, levels, margin),
        grid=(rows // LANES8,), name="stage",
        out_shape=[jax.ShapeDtypeStruct((rows, depth, cols), F32)] * 4 + [jax.ShapeDtypeStruct((4 * margin, depth, cols), F32)] * 2,
        in_specs=[pl.BlockSpec((levels, LANES8, cols), lambda i: (0, i, 0))] * 4,
        out_specs=[pl.BlockSpec((LANES8, depth, cols), lambda i: (i, 0, 0))] * 4 + [pl.BlockSpec((4 * margin, depth, cols), lambda i: (0, 0, 0))] * 2,
        compiler_params=params(16))(*natural)


def obs_kernel(levels, value_ref, precision_ref, live_ref, out_ref):
    def step(p, _):
        here = pl.ds(pl.multiple_of(p * 128, 128), 128)
        live = live_ref[0:1, here] > 0
        out_ref[p, 0:levels, :] = value_ref[:, here]
        out_ref[p, levels:2 * levels, :] = jnp.where(live, precision_ref[:, here], 0.0)
        return 0
    lax.fori_loop(0, out_ref.shape[0], step, 0)


def obs_blocks(value, precision, live):
    levels, slots = value.shape
    return pl.pallas_call(functools.partial(obs_kernel, levels), name="obs_blocks",
        out_shape=jax.ShapeDtypeStruct((slots // 128, -(-2 * levels // LANES8) * LANES8, 128), F32),
        in_specs=[WHOLE] * 3, out_specs=WHOLE, compiler_params=params(12))(value, precision, live)


def turn(x, shift):
    shift = shift % 128
    return pltpu.roll(x, shift, x.ndim - 1) if shift else x


def place(rows):
    lane = lax.broadcasted_iota(jnp.int32, (rows, LANES8, 128), 2)
    return lane, lane % (4 * STEPS)


def slabs_of(groups):
    slabs = -(-groups // 8)
    return slabs, -(-groups // slabs)


def pack_strip(load, groups, rows, margin):
    lane, _ = place(rows)
    width = 4 * margin
    west = east = jnp.zeros((rows, LANES8, 128), F32)
    for g in range(groups):
        x = load(g)
        here = (lane >= width * g) & (lane < width * (g + 1))
        west = jnp.where(here, turn(x, width * g + margin), west)
        east = jnp.where(here, turn(x, width * g + 2 * margin), east)
    return west, east


def pack_sends(strips, rows, margin):
    _, at = place(rows)
    to_east = to_west = jnp.zeros((rows, LANES8, 128), F32)
    for f, (west, east) in enumerate(strips):
        here = (at >= margin * f) & (at < margin * (f + 1))
        to_east = jnp.where(here, turn(east, margin * f - margin), to_east)
        to_west = jnp.where(here, turn(west, margin * f - margin), to_west)
    return to_east, to_west


def complete(f, west, east, from_west, from_east, rows, margin):
    _, at = place(rows)
    west = jnp.where(at < margin, turn(from_west, -margin * f), west)
    east = jnp.where(at >= 2 * margin, turn(from_east, 2 * margin - margin * f), east)
    return west, east


def slab_load(ref, at, count, slab, per, groups):
    return lambda g: ref[pl.ds(at, count), LANES8 * (slab * per + g):LANES8 * (slab * per + g + 1), :]


def strip_kernel(groups, rows, margin, *refs):
    fields, (south_in, north_in, strip_ref, to_east, to_west) = refs[:4], refs[4:]
    slabs, per = slabs_of(groups)
    def build(at, count, sources):
        for slab in range(slabs):
            strips = []
            for f in range(4):
                ref, start = sources[f]
                west, east = pack_strip(slab_load(ref, start, count, slab, per, groups), min(per, groups - slab * per), count, margin)
                strip_ref[f, 0, slab, pl.ds(at, count)] = west
                strip_ref[f, 1, slab, pl.ds(at, count)] = east
                strips.append((west, east))
            to_east[slab, pl.ds(at, count)], to_west[slab, pl.ds(at, count)] = pack_sends(strips, count, margin)
    def inside(i, _):
        build(2 * i + margin, 2, [(fields[f], 2 * i) for f in range(4)])
        return 0
    lax.fori_loop(0, rows // 2, inside, 0)
    def outside(i, _):
        build(2 * i, 2, [(south_in, f * margin + 2 * i) for f in range(4)])
        build(2 * i + margin + rows, 2, [(north_in, f * margin + 2 * i) for f in range(4)])
        return 0
    lax.fori_loop(0, margin // 2, outside, 0)


def strip_fields(groups, rows, margin, fields, south_in, north_in):
    tall = rows + 2 * margin
    slabs, _ = slabs_of(groups)
    return pl.pallas_call(functools.partial(strip_kernel, groups, rows, margin),
        out_shape=[jax.ShapeDtypeStruct((4, 2, slabs, tall, LANES8, 128), F32)] + [jax.ShapeDtypeStruct((slabs, tall, LANES8, 128), F32)] * 2,
        in_specs=[WHOLE] * 6, out_specs=[WHOLE] * 3, name="strip_fields", compiler_params=params(16))(*fields, south_in, north_in)


def faces_kernel(groups, rows, margin, mask_ref, east_ref, north_ref, south_in, north_in, e_out, n_out, mask):
    tall = rows + 2 * margin
    def step(g, _):
        put = lanes_of(g)
        mask[0:margin] = south_in[margin:2 * margin, put, :]
        mask[margin:margin + rows] = mask_ref[:, put, :]
        mask[margin + rows:tall] = north_in[margin:2 * margin, put, :]
        pieces = [(0, margin, south_in, 0), (margin + rows, margin, north_in, 0)] + [(margin + i, LANES8, None, i) for i in range(0, rows, LANES8)]
        for at, count, halo, i in pieces:
            if halo is None:
                east, north = east_ref[i:i + count, put, :], north_ref[i:i + count, put, :]
            else:
                east, north = halo[2 * margin:3 * margin, put, :], halo[3 * margin:4 * margin, put, :]
            own = mask[at:at + count]
            e_out[at:at + count, put, :] = east * own * turn(own, -1)
            n_out[at:at + count, put, :] = north * own * mask[at + 1:at + count + 1]
        return 0
    mask[tall] = jnp.zeros((LANES8, 128), F32)
    lax.fori_loop(0, groups, step, 0)


def faces(groups, rows, margin, fields, south_in, north_in):
    tall = rows + 2 * margin
    return pl.pallas_call(functools.partial(faces_kernel, groups, rows, margin),
        out_shape=[jax.ShapeDtypeStruct((tall, LANES8 * groups, 128), F32)] * 2,
        in_specs=[WHOLE] * 5, out_specs=[WHOLE] * 2, name="faces", scratch_shapes=[VMEM((tall + 1, LANES8, 128), F32)],
        compiler_params=params(12))(*fields[1:], south_in, north_in)


def sweep(source, east, north, write, low, high):
    for at in range(low, high, LANES8):
        end = min(at + LANES8, high)
        u = source(at - 1, end + 1)
        rise = north(at - 1, end) * (u[1:] - u[:-1])
        u = u[1:-1]
        run = east(at, end) * (turn(u, -1) - u)
        write(at, end, u + ((run - turn(run, 1)) + (rise[1:] - rise[:-1])))


def reader(ref, *lead):
    return lambda at, end: ref[(*lead, slice(at, end))]


def writer(ref, *lead):
    def write(at, end, value):
        ref[(*lead, slice(at, end))] = value
    return write


def all_sweeps(tall, margin, states, east, north, write):
    for k in range(margin):
        now, later = states[k % 2], states[(k + 1) % 2]
        sweep(reader(now), east, north, writer(later) if k + 1 < margin else write, k + 1, tall - 1 - k)


def strip_sweeps(rows, margin, strip_refs, faces_ref, rim):
    tall = rows + 2 * margin
    last = strip_refs[margin % 2]
    def step(slab, _):
        for side in range(2):
            states = [ref.at[side, slab] for ref in strip_refs]
            all_sweeps(tall, margin, states, reader(faces_ref, side, 0, slab), reader(faces_ref, side, 1, slab), writer(states[margin % 2]))
        for i in range(0, rows, LANES8):
            _, at = place(LANES8)
            here = slice(i + margin, i + margin + LANES8)
            rim[slab, i:i + LANES8] = jnp.where(at < margin, turn(last[1, slab, here], -margin), last[0, slab, here])
        return 0
    lax.fori_loop(0, rim.shape[0], step, 0)


def tile_sweeps(g, groups, rows, margin, states, e_ref, n_ref, rim, write):
    tall = rows + 2 * margin
    put = lanes_of(g)
    _, per = slabs_of(groups)
    slab = g // per
    shift = 128 - margin - 4 * margin * (g - slab * per)
    def finish(at, end, value):
        lane, _ = place(end - at)
        edge = pltpu.roll(rim[slab, at - margin:end - margin], shift, 2)
        write(at - margin, end - margin, jnp.where((lane < margin) | (lane >= 128 - margin), edge, value))
    all_sweeps(tall, margin, states, lambda a, b: e_ref[a:b, put, :], lambda a, b: n_ref[a:b, put, :], finish)


def fill(state, put, low, middle, high, margin, offset):
    rows = middle.shape[0]
    state[0:margin] = low[offset:offset + margin, put, :]
    state[margin:margin + rows] = middle[:, put, :]
    state[margin + rows:2 * margin + rows] = high[offset:offset + margin, put, :]


def forward_kernel(groups, rows, margin, u_ref, south_in, north_in, e_ref, n_ref, strip_ref, from_west, from_east, out_ref, faces_ref, strip_a, strip_b, mask, state_a, state_b, rim):
    tall = rows + 2 * margin
    def join(slab, _):
        for side in range(2):
            mask[side, tall] = jnp.zeros((LANES8, 128), F32)
        for at in range(0, tall, LANES8):
            here = slice(at, at + LANES8)
            for f in range(4):
                pair = complete(f, strip_ref[f, 0, slab, here], strip_ref[f, 1, slab, here], from_west[slab, here], from_east[slab, here], LANES8, margin)
                for side, value in enumerate(pair):
                    if f == 0:
                        strip_a[side, slab, here] = value
                    elif f == 1:
                        mask[side, here] = value
                    else:
                        faces_ref[side, f - 2, slab, here] = value
        for at in range(0, tall, LANES8):
            here = slice(at, at + LANES8)
            for side in range(2):
                own = mask[side, here]
                faces_ref[side, 0, slab, here] = faces_ref[side, 0, slab, here] * own * turn(own, -1)
                faces_ref[side, 1, slab, here] = faces_ref[side, 1, slab, here] * own * mask[side, at + 1:at + 1 + LANES8]
        return 0
    lax.fori_loop(0, rim.shape[0], join, 0)
    strip_sweeps(rows, margin, (strip_a, strip_b), faces_ref, rim)
    def step(g, _):
        put = lanes_of(g)
        fill(state_a, put, south_in, u_ref, north_in, margin, 0)
        def write(at, end, value):
            out_ref[at:end, put, :] = value
        tile_sweeps(g, groups, rows, margin, (state_a, state_b), e_ref, n_ref, rim, write)
        return 0
    lax.fori_loop(0, groups, step, 0)


def sweep_scratch(groups, rows, margin):
    tall = rows + 2 * margin
    slabs, _ = slabs_of(groups)
    return [VMEM((2, slabs, tall, LANES8, 128), F32)] * 2, [VMEM((tall, LANES8, 128), F32)] * 2 + [VMEM((slabs, rows, LANES8, 128), F32)]


def forward(groups, rows, margin, u, south_in, north_in, e, n, strip, from_west, from_east):
    tall = rows + 2 * margin
    slabs, _ = slabs_of(groups)
    strips, tiles = sweep_scratch(groups, rows, margin)
    return pl.pallas_call(functools.partial(forward_kernel, groups, rows, margin),
        out_shape=[jax.ShapeDtypeStruct((rows, LANES8 * groups, 128), F32), jax.ShapeDtypeStruct((2, 2, slabs, tall, LANES8, 128), F32)],
        in_specs=[WHOLE] * 8, out_specs=[WHOLE] * 2, name="forward",
        scratch_shapes=strips + [VMEM((2, tall + 1, LANES8, 128), F32)] + tiles,
        compiler_params=params(24))(u, south_in, north_in, e, n, strip, from_west, from_east)


def strip_adjoint_kernel(groups, rows, margin, adjoint_ref, south_in, north_in, strip_ref, to_east, to_west):
    quarter = (rows + 2 * margin) // 4
    slabs, per = slabs_of(groups)
    def build(ref, i, at):
        for slab in range(slabs):
            west, east = pack_strip(slab_load(ref, i, 2, slab, per, groups), min(per, groups - slab * per), 2, margin)
            strip_ref[0, slab, pl.ds(at, 2)] = west
            strip_ref[1, slab, pl.ds(at, 2)] = east
    for i in range(0, margin, 2):
        build(south_in, i, i)
        build(north_in, i, i + margin + rows)
    def inside(i, _):
        build(adjoint_ref, 2 * i, 2 * i + margin)
        return 0
    lax.fori_loop(0, rows // 2, inside, 0)
    for slab in range(slabs):
        for at in range(0, quarter, 2):
            here = [slice(at + q * quarter, at + q * quarter + 2) for q in range(4)]
            sends = pack_sends([(strip_ref[0, slab, s], strip_ref[1, slab, s]) for s in here], 2, margin)
            to_east[slab, at:at + 2], to_west[slab, at:at + 2] = sends


def strip_adjoint(groups, rows, margin, adjoint, south_in, north_in):
    tall = rows + 2 * margin
    slabs, _ = slabs_of(groups)
    return pl.pallas_call(functools.partial(strip_adjoint_kernel, groups, rows, margin),
        out_shape=[jax.ShapeDtypeStruct((2, slabs, tall, LANES8, 128), F32)] + [jax.ShapeDtypeStruct((slabs, tall // 4, LANES8, 128), F32)] * 2,
        in_specs=[WHOLE] * 3, out_specs=[WHOLE] * 3, name="strip_adjoint", compiler_params=params(12))(adjoint, south_in, north_in)


def backward_kernel(groups, levels, rows, margin, adjoint_ref, south_in, north_in, strip_ref, from_west, from_east, e_ref, n_ref, faces_ref, u_ref, mask_ref,
                    out_ref, strip_a, strip_b, state_a, state_b, rim):
    quarter = (rows + 2 * margin) // 4
    for slab in range(rim.shape[0]):
        for at in range(0, quarter, 2):
            for q in range(4):
                here = slice(at + q * quarter, at + q * quarter + 2)
                pair = complete(q, strip_ref[0, slab, here], strip_ref[1, slab, here], from_west[slab, at:at + 2], from_east[slab, at:at + 2], 2, margin)
                for side in range(2):
                    strip_a[side, slab, here] = pair[side]
    strip_sweeps(rows, margin, (strip_a, strip_b), faces_ref, rim)
    def step(g, _):
        put = lanes_of(g)
        start = group_start(g, levels)
        fill(state_a, put, south_in, adjoint_ref, north_in, margin, 0)
        def write(at, end, value):
            value = u_ref[at:end, put, :] + mask_ref[at:end, put, :] * value
            for r in range(at, end):
                out_ref[pl.ds(start * rows + r, LANES8, stride=rows), :] = value[r - at]
        tile_sweeps(g, groups, rows, margin, (state_a, state_b), e_ref, n_ref, rim, write)
        return 0
    lax.fori_loop(0, groups, step, 0)


def backward(groups, levels, rows, margin, *args):
    strips, tiles = sweep_scratch(groups, rows, margin)
    return pl.pallas_call(functools.partial(backward_kernel, groups, levels, rows, margin),
        out_shape=jax.ShapeDtypeStruct((levels * rows, 128), F32),
        in_specs=[WHOLE] * 11, out_specs=WHOLE, name="backward",
        scratch_shapes=strips + tiles, compiler_params=params(24))(*args)


def departures_kernel(groups, levels, equivalent_ref, obs_ref, out_ref, back_ref):
    def step(p, _):
        for g in range(groups):
            start = group_start(g, levels)
            here = slice(LANES8 * g, LANES8 * (g + 1))
            gap = obs_ref[p, levels + start:levels + start + LANES8, :] * (equivalent_ref[p, here, :] - obs_ref[p, start:start + LANES8, :])
            back_ref[p, here, :] = gap
            out_ref[p, start:start + LANES8, :] = gap
        return 0
    lax.fori_loop(0, out_ref.shape[0], step, 0, unroll=2)


def departures_of(groups, levels, equivalent, obs):
    return pl.pallas_call(functools.partial(departures_kernel, groups, levels),
        out_shape=[jax.ShapeDtypeStruct((equivalent.shape[0], levels, 128), F32), jax.ShapeDtypeStruct(equivalent.shape, F32)],
        in_specs=[WHOLE] * 2, out_specs=[WHOLE] * 2, name="departures", compiler_params=params(16))(equivalent, obs)


def exchange(values, share):
    blocks, levels, width = values.shape
    if share > 1:
        values = values.reshape(blocks, levels, share, -1).transpose(0, 2, 1, 3)
    values = values.reshape(blocks * share, levels, width // share)
    values = lax.all_to_all(values, ("gx", "gy"), 0, 0, tiled=True)
    if share > 1:
        values = values.reshape(blocks, share, levels, -1).transpose(0, 2, 1, 3)
    return values.reshape(blocks, levels, width)


def pass_along(axis, forth, back, cyclic):
    size = lax.axis_size(axis)
    up = [(i, (i + 1) % size) for i in range(size if cyclic else size - 1)]
    down = [(j, i) for i, j in up]
    return lax.ppermute(forth, axis, up), lax.ppermute(back, axis, down)


def body(
    control,
    east_coeff,
    north_coeff,
    ocean_mask,
    corner_cells,
    corner_weights,
    obs_value,
    obs_precision,
    slot_counts,
):
    levels, rows, cols = control.shape
    slots = corner_cells.shape[1]
    capacity = slots // lax.axis_size(("gx", "gy"))
    share = 128 // capacity
    margin = STEPS
    live = (slot_counts[0][:, None] > jnp.arange(capacity)[None, :]).astype(jnp.int32).reshape(1, slots)
    groups = -(-levels // 16) * 2
    obs = exchange(obs_blocks(obs_value, obs_precision, live), share)
    *fields, top, bottom = stage(groups, margin, (control, east_coeff, north_coeff, ocean_mask))
    south_in, north_in = pass_along("gy", top, bottom, False)
    strip, to_east, to_west = strip_fields(groups, rows, margin, fields, south_in, north_in)
    from_west, from_east = pass_along("gx", to_east, to_west, True)
    e, n = faces(groups, rows, margin, fields, south_in, north_in)
    background, strip_faces = forward(groups, rows, margin, fields[0], south_in, north_in, e, n, strip, from_west, from_east)
    equivalent = gather(corner_cells, corner_weights, background, slots)
    out, back = departures_of(groups, levels, equivalent, obs)
    departures = exchange(out, share).transpose(1, 0, 2).reshape(levels, slots)
    adjoint = scatter(corner_cells, corner_weights, back, rows, cols)
    south_in, north_in = pass_along("gy", adjoint[rows - margin:], adjoint[:margin], False)
    strip, to_east, to_west = strip_adjoint(groups, rows, margin, adjoint, south_in, north_in)
    from_west, from_east = pass_along("gx", to_east, to_west, True)
    gradient = backward(groups, levels, rows, margin, adjoint, south_in, north_in, strip, from_west, from_east, e, n, strip_faces, fields[0], fields[1])
    return gradient.reshape(levels, rows, cols), departures


def solution(mesh):
    return jax.shard_map(
        body,
        mesh=mesh,
        in_specs=(
            P(None, "gy", "gx"),
            P(None, "gy", "gx"),
            P(None, "gy", "gx"),
            P(None, "gy", "gx"),
            P(None, ("gx", "gy")),
            P(None, ("gx", "gy")),
            P(None, ("gx", "gy")),
            P(None, ("gx", "gy")),
            P(("gx", "gy"), None),
        ),
        out_specs=(P(None, "gy", "gx"), P(None, ("gx", "gy"))),
        check_vma=False,
    )
```

```python
import functools

import jax
import jax.numpy as jnp
from jax import lax
from jax.experimental import pallas as pl
from jax.experimental.pallas import tpu as pltpu
from jax.sharding import PartitionSpec as P


F32, BF16 = jnp.float32, jnp.bfloat16
VMEM = pltpu.VMEM
STEPS = 4
LANES8 = 8
WHOLE = pl.BlockSpec(memory_space=pltpu.VMEM)


def split2(x):
    hi = x.astype(BF16)
    lo = (x - hi.astype(F32)).astype(BF16)
    return hi, lo


def hats(cells_ref, weights_ref, j0, n, cols):
    c = cells_ref[0:1, pl.ds(j0, n)]
    w = weights_ref[:, pl.ds(j0, n)]
    r = c // cols
    s = c - r * cols
    east, west = w[1:2] + w[3:4], w[0:1] + w[2:3]
    north, south = w[2:3] + w[3:4], w[0:1] + w[1:2]
    return r, s, east, west, north, south


def hat(index, low, high, size):
    at = lax.broadcasted_iota(jnp.int32, (size, index.shape[1]), 0) - index
    return jnp.where(at == 0, low, jnp.where(at == 1, high, 0.0))


def gather_kernel(rows, lev, cols, nb, cells_ref, weights_ref, bg_ref, out_ref, bb, t0, t1, rr0, rr1):
    for r in range(rows):
        hi, lo = split2(bg_ref[r])
        bb[r * lev:(r + 1) * lev, 0:cols] = hi
        bb[r * lev:(r + 1) * lev, cols:2 * cols] = lo
    blk = 256
    def multiply(jb, t, rr):
        r, s, east, west, north, south = hats(cells_ref, weights_ref, pl.multiple_of(jb * blk, blk), blk, cols)
        rr[...] = hat(r, south, north, rows)
        hi, lo = split2(hat(s, west, east, cols))
        left = bb[...]
        t[...] = (jnp.dot(left, jnp.concatenate([hi, hi], 0), preferred_element_type=F32)
                  + jnp.dot(left, jnp.concatenate([lo, lo], 0), preferred_element_type=F32))
    def reduce(jb, t, rr):
        acc = jnp.zeros((lev, blk), F32)
        for r in range(rows):
            acc = acc + t[r * lev:(r + 1) * lev, :] * rr[r:r + 1, :]
        out_ref[2 * jb] = acc[:, 0:128]
        out_ref[2 * jb + 1] = acc[:, 128:256]
    def step(i, _):
        multiply(2 * i, t0, rr0)
        multiply(2 * i + 1, t1, rr1)
        reduce(2 * i, t0, rr0)
        reduce(2 * i + 1, t1, rr1)
        return 0
    lax.fori_loop(0, nb // 2, step, 0)


def gather(cells, weights, bg, slots):
    rows, lev, cols = bg.shape
    nb = slots // 256
    return pl.pallas_call(functools.partial(gather_kernel, rows, lev, cols, nb),
        out_shape=jax.ShapeDtypeStruct((2 * nb, lev, 128), F32),
        in_specs=[pl.BlockSpec(memory_space=VMEM)] * 3,
        out_specs=pl.BlockSpec(memory_space=VMEM), name="gather",
        scratch_shapes=[VMEM((rows * lev, 2 * cols), BF16), VMEM((rows * lev, 256), F32), VMEM((rows * lev, 256), F32), VMEM((rows, 256), F32), VMEM((rows, 256), F32)],
        compiler_params=params(20),
    )(cells, weights, bg)


def scatter_kernel(rows, lev, cols, nb, cells_ref, weights_ref, back_ref, out_ref, x, acc):
    blk = 256
    acc[...] = jnp.zeros_like(acc)
    def step(jb, _):
        r, s, east, west, north, south = hats(cells_ref, weights_ref, pl.multiple_of(jb * blk, blk), blk, cols)
        hi, lo = split2(hat(s, west, east, cols))
        right = jnp.concatenate([hi, lo], 0)
        back = jnp.concatenate([back_ref[2 * jb], back_ref[2 * jb + 1]], 1)
        u_hi, u_lo = split2(back * south)
        v_hi, v_lo = split2(back * north)
        one = hat(r, 1.0, 0.0, rows + 1).astype(BF16)
        for q in range(rows):
            at = jnp.broadcast_to(one[q:q + 1, :], (lev, blk))
            if q:
                below = jnp.broadcast_to(one[q - 1:q, :], (lev, blk))
                x[q * lev:(q + 1) * lev, 0:blk] = u_hi * at + v_hi * below
                x[q * lev:(q + 1) * lev, blk:] = u_lo * at + v_lo * below
            else:
                x[0:lev, 0:blk] = u_hi * at
                x[0:lev, blk:] = u_lo * at
        acc[...] += lax.dot_general(x[...], jnp.concatenate([right, right], 1), (((1,), (1,)), ((), ())), preferred_element_type=F32)
        return 0
    lax.fori_loop(0, nb, step, 0)
    for r in range(rows):
        a = acc[r * lev:(r + 1) * lev, :]
        out_ref[r] = a[:, 0:cols] + a[:, cols:]


def scatter(cells, weights, back, rows, cols):
    n2, lev, _ = back.shape
    nb = n2 // 2
    return pl.pallas_call(functools.partial(scatter_kernel, rows, lev, cols, nb),
        out_shape=jax.ShapeDtypeStruct((rows, lev, cols), F32),
        in_specs=[pl.BlockSpec(memory_space=VMEM)] * 3,
        out_specs=pl.BlockSpec(memory_space=VMEM), name="scatter",
        scratch_shapes=[VMEM((rows * lev, 512), BF16), VMEM((rows * lev, 256), F32)],
        compiler_params=params(20),
    )(cells, weights, back)


def group_start(g, levels):
    start, last = LANES8 * g, levels - LANES8
    return min(start, last) if isinstance(g, int) else jnp.minimum(start, last)


def params(megabytes):
    return pltpu.CompilerParams(vmem_limit_bytes=megabytes * 2**20)


def lanes_of(g):
    return pl.ds(pl.multiple_of(LANES8 * g, LANES8), LANES8)


def obs_kernel(levels, value_ref, precision_ref, live_ref, out_ref):
    def step(p, _):
        here = pl.ds(pl.multiple_of(p * 128, 128), 128)
        live = live_ref[0:1, here] > 0
        out_ref[p, 0:levels, :] = value_ref[:, here]
        out_ref[p, levels:2 * levels, :] = jnp.where(live, precision_ref[:, here], 0.0)
        return 0
    lax.fori_loop(0, out_ref.shape[0], step, 0)


def obs_blocks(value, precision, live):
    levels, slots = value.shape
    return pl.pallas_call(functools.partial(obs_kernel, levels), name="obs_blocks",
        out_shape=jax.ShapeDtypeStruct((slots // 128, -(-2 * levels // LANES8) * LANES8, 128), F32),
        in_specs=[WHOLE] * 3, out_specs=WHOLE, compiler_params=params(12))(value, precision, live)


def turn(x, shift):
    shift = shift % 128
    return pltpu.roll(x, shift, x.ndim - 1) if shift else x


def place(rows):
    lane = lax.broadcasted_iota(jnp.int32, (rows, LANES8, 128), 2)
    return lane, lane % (4 * STEPS)


def slabs_of(groups):
    slabs = -(-groups // 8)
    return slabs, -(-groups // slabs)


def pack_strip(load, groups, rows, margin):
    lane, _ = place(rows)
    width = 4 * margin
    west = east = jnp.zeros((rows, LANES8, 128), F32)
    for g in range(groups):
        x = load(g)
        here = (lane >= width * g) & (lane < width * (g + 1))
        west = jnp.where(here, turn(x, width * g + margin), west)
        east = jnp.where(here, turn(x, width * g + 2 * margin), east)
    return west, east


def pack_sends(strips, rows, margin):
    _, at = place(rows)
    to_east = to_west = jnp.zeros((rows, LANES8, 128), F32)
    for f, (west, east) in enumerate(strips):
        here = (at >= margin * f) & (at < margin * (f + 1))
        to_east = jnp.where(here, turn(east, margin * f - margin), to_east)
        to_west = jnp.where(here, turn(west, margin * f - margin), to_west)
    return to_east, to_west


def complete(f, west, east, from_west, from_east, rows, margin):
    _, at = place(rows)
    west = jnp.where(at < margin, turn(from_west, -margin * f), west)
    east = jnp.where(at >= 2 * margin, turn(from_east, 2 * margin - margin * f), east)
    return west, east


def slab_load(ref, at, count, slab, per):
    return lambda g: ref[pl.ds(at, count), LANES8 * (slab * per + g):LANES8 * (slab * per + g + 1), :]


def stage_kernel(groups, levels, margin, control_ref, east_ref, north_ref, mask_ref, *outs):
    cols = control_ref.shape[2]
    refs = [ref.reshape(levels * LANES8, cols) for ref in (control_ref, east_ref, north_ref, mask_ref)]
    block, last = pl.program_id(0), pl.num_programs(0) - 1
    field_refs, (top_ref, bottom_ref, strip_ref) = outs[:4], outs[4:]
    def step(g, _):
        start = group_start(g, levels)
        for r in range(LANES8):
            where = pl.ds(start * LANES8 + r, LANES8, stride=LANES8)
            control, east, north, mask = (ref[where, :] for ref in refs)
            mask = mask.astype(F32)
            for ref, value in zip(field_refs, (mask * control, mask, east, north)):
                ref[r, lanes_of(g), :] = value
        return 0
    lax.fori_loop(0, groups, step, 0)
    slabs, per = slabs_of(groups)
    count = 2
    def pack(i, _):
        at = count * i
        for slab in range(slabs):
            for f in range(4):
                west, east = pack_strip(slab_load(field_refs[f], at, count, slab, per), min(per, groups - slab * per), count, margin)
                strip_ref[f, 0, slab, pl.ds(at, count)] = west
                strip_ref[f, 1, slab, pl.ds(at, count)] = east
        return 0
    lax.fori_loop(0, LANES8 // count, pack, 0)
    @pl.when(block == 0)
    def _():
        for f in range(4):
            bottom_ref[f * margin:(f + 1) * margin] = field_refs[f][0:margin]
    @pl.when(block == last)
    def _():
        for f in range(4):
            top_ref[f * margin:(f + 1) * margin] = field_refs[f][LANES8 - margin:LANES8]


def stage(groups, margin, natural):
    levels, rows, cols = natural[0].shape
    depth = LANES8 * groups
    slabs, _ = slabs_of(groups)
    natural = [pltpu.with_memory_space_constraint(x, pltpu.HBM) for x in natural]
    return pl.pallas_call(functools.partial(stage_kernel, groups, levels, margin),
        grid=(rows // LANES8,), name="stage",
        out_shape=[jax.ShapeDtypeStruct((rows, depth, cols), F32)] * 4 + [jax.ShapeDtypeStruct((4 * margin, depth, cols), F32)] * 2
        + [jax.ShapeDtypeStruct((4, 2, slabs, rows, LANES8, 128), F32)],
        in_specs=[pl.BlockSpec((levels, LANES8, cols), lambda i: (0, i, 0))] * 4,
        out_specs=[pl.BlockSpec((LANES8, depth, cols), lambda i: (i, 0, 0))] * 4 + [pl.BlockSpec((4 * margin, depth, cols), lambda i: (0, 0, 0))] * 2
        + [pl.BlockSpec((4, 2, slabs, LANES8, LANES8, 128), lambda i: (0, 0, 0, i, 0, 0))],
        compiler_params=params(16))(*natural)


def sends_kernel(groups, levels, margin, control_ref, east_ref, north_ref, mask_ref, to_east, to_west):
    cols = control_ref.shape[2]
    refs = [ref.reshape(levels * LANES8, cols) for ref in (control_ref, east_ref, north_ref, mask_ref)]
    slabs, per = slabs_of(groups)
    quad = lax.broadcasted_iota(jnp.int32, (LANES8, 128), 1) // margin
    for r in range(LANES8):
        for slab in range(slabs):
            east_out = west_out = jnp.zeros((LANES8, 128), F32)
            for g in range(min(per, groups - slab * per)):
                where = pl.ds(group_start(slab * per + g, levels) * LANES8 + r, LANES8, stride=LANES8)
                control, east, north, mask = (ref[where, :] for ref in refs)
                mask = mask.astype(F32)
                for f, x in enumerate((mask * control, mask, east, north)):
                    here = quad == 4 * g + f
                    east_out = jnp.where(here, turn(x, margin * (4 * g + f + 1) - cols), east_out)
                    west_out = jnp.where(here, turn(x, margin * (4 * g + f)), west_out)
            to_east[slab, r] = east_out
            to_west[slab, r] = west_out


def lon_sends(groups, margin, natural):
    levels, rows, cols = natural[0].shape
    slabs, _ = slabs_of(groups)
    natural = [pltpu.with_memory_space_constraint(x, pltpu.HBM) for x in natural]
    return pl.pallas_call(functools.partial(sends_kernel, groups, levels, margin), grid=(rows // LANES8,), name="lon_sends",
        out_shape=[jax.ShapeDtypeStruct((slabs, rows, LANES8, 128), F32)] * 2,
        in_specs=[pl.BlockSpec((levels, LANES8, cols), lambda i: (0, i, 0))] * 4,
        out_specs=[pl.BlockSpec((slabs, LANES8, LANES8, 128), lambda i: (0, i, 0, 0))] * 2,
        compiler_params=params(16))(*natural)


def rim_kernel(groups, margin, south_in, north_in, strip_ref):
    slabs, per = slabs_of(groups)
    for slab in range(slabs):
        for f in range(4):
            for end, ref in enumerate((south_in, north_in)):
                west, east = pack_strip(slab_load(ref, f * margin, margin, slab, per), min(per, groups - slab * per), margin, margin)
                strip_ref[f, 0, slab, end * margin:(end + 1) * margin] = west
                strip_ref[f, 1, slab, end * margin:(end + 1) * margin] = east


def strip_rims(groups, margin, south_in, north_in):
    slabs, _ = slabs_of(groups)
    return pl.pallas_call(functools.partial(rim_kernel, groups, margin),
        out_shape=jax.ShapeDtypeStruct((4, 2, slabs, 2 * margin, LANES8, 128), F32),
        in_specs=[WHOLE] * 2, out_specs=WHOLE, name="strip_rims", compiler_params=params(12))(south_in, north_in)


def faces_kernel(groups, rows, margin, mask_ref, east_ref, north_ref, south_in, north_in, e_out, n_out, mask):
    tall = rows + 2 * margin
    def step(g, _):
        put = lanes_of(g)
        mask[0:margin] = south_in[margin:2 * margin, put, :]
        mask[margin:margin + rows] = mask_ref[:, put, :]
        mask[margin + rows:tall] = north_in[margin:2 * margin, put, :]
        pieces = [(0, margin, south_in, 0), (margin + rows, margin, north_in, 0)] + [(margin + i, LANES8, None, i) for i in range(0, rows, LANES8)]
        for at, count, halo, i in pieces:
            if halo is None:
                east, north = east_ref[i:i + count, put, :], north_ref[i:i + count, put, :]
            else:
                east, north = halo[2 * margin:3 * margin, put, :], halo[3 * margin:4 * margin, put, :]
            own = mask[at:at + count]
            e_out[at:at + count, put, :] = east * own * turn(own, -1)
            n_out[at:at + count, put, :] = north * own * mask[at + 1:at + count + 1]
        return 0
    mask[tall] = jnp.zeros((LANES8, 128), F32)
    lax.fori_loop(0, groups, step, 0)


def faces(groups, rows, margin, fields, south_in, north_in):
    tall = rows + 2 * margin
    return pl.pallas_call(functools.partial(faces_kernel, groups, rows, margin),
        out_shape=[jax.ShapeDtypeStruct((tall, LANES8 * groups, 128), F32)] * 2,
        in_specs=[WHOLE] * 5, out_specs=[WHOLE] * 2, name="faces", scratch_shapes=[VMEM((tall + 1, LANES8, 128), F32)],
        compiler_params=params(12))(*fields[1:], south_in, north_in)


def sweep(source, east, north, write, low, high):
    for at in range(low, high, LANES8):
        end = min(at + LANES8, high)
        u = source(at - 1, end + 1)
        rise = north(at - 1, end) * (u[1:] - u[:-1])
        u = u[1:-1]
        run = east(at, end) * (turn(u, -1) - u)
        write(at, end, u + ((run - turn(run, 1)) + (rise[1:] - rise[:-1])))


def reader(ref, *lead):
    return lambda at, end: ref[(*lead, slice(at, end))]


def writer(ref, *lead):
    def write(at, end, value):
        ref[(*lead, slice(at, end))] = value
    return write


def all_sweeps(tall, margin, states, east, north, write):
    for k in range(margin):
        now, later = states[k % 2], states[(k + 1) % 2]
        sweep(reader(now), east, north, writer(later) if k + 1 < margin else write, k + 1, tall - 1 - k)


def strip_sweeps(rows, margin, strip_refs, faces_ref, rim):
    tall = rows + 2 * margin
    last = strip_refs[margin % 2]
    def step(slab, _):
        for side in range(2):
            states = [ref.at[side, slab] for ref in strip_refs]
            all_sweeps(tall, margin, states, reader(faces_ref, side, 0, slab), reader(faces_ref, side, 1, slab), writer(states[margin % 2]))
        for i in range(0, rows, LANES8):
            _, at = place(LANES8)
            here = slice(i + margin, i + margin + LANES8)
            rim[slab, i:i + LANES8] = jnp.where(at < margin, turn(last[1, slab, here], -margin), last[0, slab, here])
        return 0
    lax.fori_loop(0, rim.shape[0], step, 0)


def tile_sweeps(g, groups, rows, margin, states, e_ref, n_ref, rim, write):
    tall = rows + 2 * margin
    put = lanes_of(g)
    _, per = slabs_of(groups)
    slab = g // per
    shift = 128 - margin - 4 * margin * (g - slab * per)
    def finish(at, end, value):
        lane, _ = place(end - at)
        edge = pltpu.roll(rim[slab, at - margin:end - margin], shift, 2)
        write(at - margin, end - margin, jnp.where((lane < margin) | (lane >= 128 - margin), edge, value))
    all_sweeps(tall, margin, states, lambda a, b: e_ref[a:b, put, :], lambda a, b: n_ref[a:b, put, :], finish)


def fill(state, put, low, middle, high, margin, offset):
    rows = middle.shape[0]
    state[0:margin] = low[offset:offset + margin, put, :]
    state[margin:margin + rows] = middle[:, put, :]
    state[margin + rows:2 * margin + rows] = high[offset:offset + margin, put, :]


def forward_kernel(groups, rows, margin, u_ref, south_in, north_in, e_ref, n_ref, strip_ref, from_west, from_east, rims_ref, south_corners, north_corners, out_ref, faces_ref, strip_a, strip_b, mask, state_a, state_b, rim):
    tall = rows + 2 * margin
    def join(slab, _):
        for side in range(2):
            mask[side, tall] = jnp.zeros((LANES8, 128), F32)
        pieces = [(0, margin, rims_ref, 0, south_corners.at[0, slab], south_corners.at[1, slab], 0),
                  (margin + rows, margin, rims_ref, margin, north_corners.at[0, slab], north_corners.at[1, slab], 0)]
        pieces += [(margin + i, LANES8, strip_ref, i, from_west.at[slab], from_east.at[slab], i) for i in range(0, rows, LANES8)]
        for at, count, own_ref, own_at, west_ref, east_ref, in_at in pieces:
            here, there, source = slice(at, at + count), slice(own_at, own_at + count), slice(in_at, in_at + count)
            for f in range(4):
                pair = complete(f, own_ref[f, 0, slab, there], own_ref[f, 1, slab, there], west_ref[source], east_ref[source], count, margin)
                for side, value in enumerate(pair):
                    if f == 0:
                        strip_a[side, slab, here] = value
                    elif f == 1:
                        mask[side, here] = value
                    else:
                        faces_ref[side, f - 2, slab, here] = value
        for at in range(0, tall, LANES8):
            here = slice(at, at + LANES8)
            for side in range(2):
                own = mask[side, here]
                faces_ref[side, 0, slab, here] = faces_ref[side, 0, slab, here] * own * turn(own, -1)
                faces_ref[side, 1, slab, here] = faces_ref[side, 1, slab, here] * own * mask[side, at + 1:at + 1 + LANES8]
        return 0
    lax.fori_loop(0, rim.shape[0], join, 0)
    strip_sweeps(rows, margin, (strip_a, strip_b), faces_ref, rim)
    def step(g, _):
        put = lanes_of(g)
        fill(state_a, put, south_in, u_ref, north_in, margin, 0)
        def write(at, end, value):
            out_ref[at:end, put, :] = value
        tile_sweeps(g, groups, rows, margin, (state_a, state_b), e_ref, n_ref, rim, write)
        return 0
    lax.fori_loop(0, groups, step, 0)


def sweep_scratch(groups, rows, margin):
    tall = rows + 2 * margin
    slabs, _ = slabs_of(groups)
    return [VMEM((2, slabs, tall, LANES8, 128), F32)] * 2, [VMEM((tall, LANES8, 128), F32)] * 2 + [VMEM((slabs, rows, LANES8, 128), F32)]


def forward(groups, rows, margin, *args):
    tall = rows + 2 * margin
    slabs, _ = slabs_of(groups)
    strips, tiles = sweep_scratch(groups, rows, margin)
    return pl.pallas_call(functools.partial(forward_kernel, groups, rows, margin),
        out_shape=[jax.ShapeDtypeStruct((rows, LANES8 * groups, 128), F32), jax.ShapeDtypeStruct((2, 2, slabs, tall, LANES8, 128), F32)],
        in_specs=[WHOLE] * 11, out_specs=[WHOLE] * 2, name="forward",
        scratch_shapes=strips + [VMEM((2, tall + 1, LANES8, 128), F32)] + tiles,
        compiler_params=params(24))(*args)


def strip_adjoint_kernel(groups, rows, margin, adjoint_ref, south_in, north_in, strip_ref, to_east, to_west):
    quarter = (rows + 2 * margin) // 4
    slabs, per = slabs_of(groups)
    def build(ref, i, at):
        for slab in range(slabs):
            west, east = pack_strip(slab_load(ref, i, 2, slab, per), min(per, groups - slab * per), 2, margin)
            strip_ref[0, slab, pl.ds(at, 2)] = west
            strip_ref[1, slab, pl.ds(at, 2)] = east
    for i in range(0, margin, 2):
        build(south_in, i, i)
        build(north_in, i, i + margin + rows)
    def inside(i, _):
        build(adjoint_ref, 2 * i, 2 * i + margin)
        return 0
    lax.fori_loop(0, rows // 2, inside, 0)
    for slab in range(slabs):
        for at in range(0, quarter, 2):
            here = [slice(at + q * quarter, at + q * quarter + 2) for q in range(4)]
            sends = pack_sends([(strip_ref[0, slab, s], strip_ref[1, slab, s]) for s in here], 2, margin)
            to_east[slab, at:at + 2], to_west[slab, at:at + 2] = sends


def strip_adjoint(groups, rows, margin, adjoint, south_in, north_in):
    tall = rows + 2 * margin
    slabs, _ = slabs_of(groups)
    return pl.pallas_call(functools.partial(strip_adjoint_kernel, groups, rows, margin),
        out_shape=[jax.ShapeDtypeStruct((2, slabs, tall, LANES8, 128), F32)] + [jax.ShapeDtypeStruct((slabs, tall // 4, LANES8, 128), F32)] * 2,
        in_specs=[WHOLE] * 3, out_specs=[WHOLE] * 3, name="strip_adjoint", compiler_params=params(12))(adjoint, south_in, north_in)


def backward_kernel(groups, levels, rows, margin, adjoint_ref, south_in, north_in, strip_ref, from_west, from_east, e_ref, n_ref, faces_ref, u_ref, mask_ref,
                    out_ref, strip_a, strip_b, state_a, state_b, rim):
    quarter = (rows + 2 * margin) // 4
    for slab in range(rim.shape[0]):
        for at in range(0, quarter, 2):
            for q in range(4):
                here = slice(at + q * quarter, at + q * quarter + 2)
                pair = complete(q, strip_ref[0, slab, here], strip_ref[1, slab, here], from_west[slab, at:at + 2], from_east[slab, at:at + 2], 2, margin)
                for side in range(2):
                    strip_a[side, slab, here] = pair[side]
    strip_sweeps(rows, margin, (strip_a, strip_b), faces_ref, rim)
    def step(g, _):
        put = lanes_of(g)
        start = group_start(g, levels)
        fill(state_a, put, south_in, adjoint_ref, north_in, margin, 0)
        def write(at, end, value):
            value = u_ref[at:end, put, :] + mask_ref[at:end, put, :] * value
            for r in range(at, end):
                out_ref[pl.ds(start * rows + r, LANES8, stride=rows), :] = value[r - at]
        tile_sweeps(g, groups, rows, margin, (state_a, state_b), e_ref, n_ref, rim, write)
        return 0
    lax.fori_loop(0, groups, step, 0)


def backward(groups, levels, rows, margin, *args):
    strips, tiles = sweep_scratch(groups, rows, margin)
    return pl.pallas_call(functools.partial(backward_kernel, groups, levels, rows, margin),
        out_shape=jax.ShapeDtypeStruct((levels * rows, 128), F32),
        in_specs=[WHOLE] * 11, out_specs=WHOLE, name="backward",
        scratch_shapes=strips + tiles, compiler_params=params(24))(*args)


def departures_kernel(groups, levels, equivalent_ref, obs_ref, out_ref, back_ref):
    def step(p, _):
        for g in range(groups):
            start = group_start(g, levels)
            here = slice(LANES8 * g, LANES8 * (g + 1))
            gap = obs_ref[p, levels + start:levels + start + LANES8, :] * (equivalent_ref[p, here, :] - obs_ref[p, start:start + LANES8, :])
            back_ref[p, here, :] = gap
            out_ref[p, start:start + LANES8, :] = gap
        return 0
    lax.fori_loop(0, out_ref.shape[0], step, 0, unroll=2)


def departures_of(groups, levels, equivalent, obs):
    return pl.pallas_call(functools.partial(departures_kernel, groups, levels),
        out_shape=[jax.ShapeDtypeStruct((equivalent.shape[0], levels, 128), F32), jax.ShapeDtypeStruct(equivalent.shape, F32)],
        in_specs=[WHOLE] * 2, out_specs=[WHOLE] * 2, name="departures", compiler_params=params(16))(equivalent, obs)


def place_kernel(part_ref, out_ref):
    def step(p, _):
        out_ref[:, pl.ds(pl.multiple_of(p * 128, 128), 128)] = part_ref[p]
        return 0
    lax.fori_loop(0, part_ref.shape[0], step, 0, unroll=2)


def place_departures(part):
    blocks, levels, width = part.shape
    return pl.pallas_call(place_kernel, name="place_departures",
        out_shape=jax.ShapeDtypeStruct((levels, blocks * width), F32),
        in_specs=[WHOLE], out_specs=WHOLE, compiler_params=params(12))(part)


def exchange(values, share):
    blocks, levels, width = values.shape
    if share > 1:
        values = values.reshape(blocks, levels, share, -1).transpose(0, 2, 1, 3)
    values = values.reshape(blocks * share, levels, width // share)
    values = lax.all_to_all(values, ("gx", "gy"), 0, 0, tiled=True)
    if share > 1:
        values = values.reshape(blocks, share, levels, -1).transpose(0, 2, 1, 3)
    return values.reshape(blocks, levels, width)


def pass_around(axis, forth, back):
    size = lax.axis_size(axis)
    up = [(i, (i + 1) % size) for i in range(size)]
    return lax.ppermute(forth, axis, up), lax.ppermute(back, axis, [(j, i) for i, j in up])


def swap_edges(axis, forth, back):
    size, odd = lax.axis_size(axis), lax.axis_index(axis) % 2 == 1
    rounds = [[pair for i in range(first, size - 1, 2) for pair in ((i, i + 1), (i + 1, i))] for first in range(2)]
    inner = lax.ppermute(jnp.where(odd, back, forth), axis, rounds[0])
    outer = lax.ppermute(jnp.where(odd, forth, back), axis, rounds[1])
    return jnp.where(odd, inner, outer), jnp.where(odd, outer, inner)


def body(
    control,
    east_coeff,
    north_coeff,
    ocean_mask,
    corner_cells,
    corner_weights,
    obs_value,
    obs_precision,
    slot_counts,
):
    levels, rows, cols = control.shape
    slots = corner_cells.shape[1]
    capacity = slots // lax.axis_size(("gx", "gy"))
    share = 128 // capacity
    margin = STEPS
    live = (slot_counts[0][:, None] > jnp.arange(capacity)[None, :]).astype(jnp.int32).reshape(1, slots)
    groups = -(-levels // 16) * 2
    natural = (control, east_coeff, north_coeff, ocean_mask)
    to_east, to_west = lon_sends(groups, margin, natural)
    from_west, from_east = pass_around("gx", to_east, to_west)
    obs = obs_blocks(obs_value, obs_precision, live)
    obs, *_ = lax.optimization_barrier((obs, to_east, to_west))
    obs = exchange(obs, share)
    *fields, top, bottom, strip = stage(groups, margin, natural)
    south_in, north_in = swap_edges("gy", top, bottom)
    corners = jnp.stack([from_west, from_east])
    south_corners, north_corners = swap_edges("gy", corners[:, :, rows - margin:], corners[:, :, :margin])
    rims = strip_rims(groups, margin, south_in, north_in)
    e, n = faces(groups, rows, margin, fields, south_in, north_in)
    background, strip_faces = forward(groups, rows, margin, fields[0], south_in, north_in, e, n, strip, from_west, from_east, rims, south_corners, north_corners)
    equivalent = gather(corner_cells, corner_weights, background, slots)
    out, back = departures_of(groups, levels, equivalent, obs)
    sent = exchange(out, share)
    adjoint = scatter(corner_cells, corner_weights, back, rows, cols)
    south_in, north_in = swap_edges("gy", adjoint[rows - margin:], adjoint[:margin])
    strip, to_east, to_west = strip_adjoint(groups, rows, margin, adjoint, south_in, north_in)
    from_west, from_east = pass_around("gx", to_east, to_west)
    departures = place_departures(sent)
    gradient = backward(groups, levels, rows, margin, adjoint, south_in, north_in, strip, from_west, from_east, e, n, strip_faces, fields[0], fields[1])
    return gradient.reshape(levels, rows, cols), departures


def solution(mesh):
    return jax.shard_map(
        body,
        mesh=mesh,
        in_specs=(
            P(None, "gy", "gx"),
            P(None, "gy", "gx"),
            P(None, "gy", "gx"),
            P(None, "gy", "gx"),
            P(None, ("gx", "gy")),
            P(None, ("gx", "gy")),
            P(None, ("gx", "gy")),
            P(None, ("gx", "gy")),
            P(("gx", "gy"), None),
        ),
        out_specs=(P(None, "gy", "gx"), P(None, ("gx", "gy"))),
        check_vma=False,
    )
```

```python
import functools

import jax
import jax.numpy as jnp
from jax import lax
from jax.experimental import pallas as pl
from jax.experimental.pallas import tpu as pltpu
from jax.sharding import PartitionSpec as P


F32, BF16 = jnp.float32, jnp.bfloat16
VMEM = pltpu.VMEM
STEPS = 4
LANES8 = 8
WHOLE = pl.BlockSpec(memory_space=pltpu.VMEM)


def split2(x):
    hi = x.astype(BF16)
    lo = (x - hi.astype(F32)).astype(BF16)
    return hi, lo


def hats(cells_ref, weights_ref, j0, n, cols):
    c = cells_ref[0:1, pl.ds(j0, n)]
    w = weights_ref[:, pl.ds(j0, n)]
    r = c // cols
    s = c - r * cols
    east, west = w[1:2] + w[3:4], w[0:1] + w[2:3]
    north, south = w[2:3] + w[3:4], w[0:1] + w[1:2]
    return r, s, east, west, north, south


def hat(index, low, high, size):
    at = lax.broadcasted_iota(jnp.int32, (size, index.shape[1]), 0) - index
    return jnp.where(at == 0, low, jnp.where(at == 1, high, 0.0))


def gather_kernel(rows, lev, cols, nb, margin, cells_ref, weights_ref, bg_ref, rim_ref, out_ref, bb, t0, t1, rr0, rr1):
    for r in range(rows):
        parts = [put_rim(bg_ref[r, 8 * g:8 * g + 8, :], g, lev // 8, margin, lambda slab: rim_ref[slab, r]) for g in range(lev // 8)]
        hi, lo = split2(jnp.concatenate(parts, 0))
        bb[r * lev:(r + 1) * lev, 0:cols] = hi
        bb[r * lev:(r + 1) * lev, cols:2 * cols] = lo
    blk = 256
    def multiply(jb, t, rr):
        r, s, east, west, north, south = hats(cells_ref, weights_ref, pl.multiple_of(jb * blk, blk), blk, cols)
        rr[...] = hat(r, south, north, rows)
        hi, lo = split2(hat(s, west, east, cols))
        left = bb[...]
        t[...] = (jnp.dot(left, jnp.concatenate([hi, hi], 0), preferred_element_type=F32)
                  + jnp.dot(left, jnp.concatenate([lo, lo], 0), preferred_element_type=F32))
    def reduce(jb, t, rr):
        acc = jnp.zeros((lev, blk), F32)
        for r in range(rows):
            acc = acc + t[r * lev:(r + 1) * lev, :] * rr[r:r + 1, :]
        out_ref[2 * jb] = acc[:, 0:128]
        out_ref[2 * jb + 1] = acc[:, 128:256]
    def step(i, _):
        multiply(2 * i, t0, rr0)
        multiply(2 * i + 1, t1, rr1)
        reduce(2 * i, t0, rr0)
        reduce(2 * i + 1, t1, rr1)
        return 0
    lax.fori_loop(0, nb // 2, step, 0)


def gather(cells, weights, bg, rim, slots, margin):
    rows, lev, cols = bg.shape
    nb = slots // 256
    return pl.pallas_call(functools.partial(gather_kernel, rows, lev, cols, nb, margin),
        out_shape=jax.ShapeDtypeStruct((2 * nb, lev, 128), F32),
        in_specs=[pl.BlockSpec(memory_space=VMEM)] * 4,
        out_specs=pl.BlockSpec(memory_space=VMEM), name="gather",
        scratch_shapes=[VMEM((rows * lev, 2 * cols), BF16), VMEM((rows * lev, 256), F32), VMEM((rows * lev, 256), F32), VMEM((rows, 256), F32), VMEM((rows, 256), F32)],
        compiler_params=params(20),
    )(cells, weights, bg, rim)


def scatter_kernel(rows, lev, cols, nb, cells_ref, weights_ref, back_ref, out_ref, x, acc):
    blk = 256
    acc[...] = jnp.zeros_like(acc)
    def step(jb, _):
        r, s, east, west, north, south = hats(cells_ref, weights_ref, pl.multiple_of(jb * blk, blk), blk, cols)
        hi, lo = split2(hat(s, west, east, cols))
        right = jnp.concatenate([hi, lo], 0)
        back = jnp.concatenate([back_ref[2 * jb], back_ref[2 * jb + 1]], 1)
        u_hi, u_lo = split2(back * south)
        v_hi, v_lo = split2(back * north)
        one = hat(r, 1.0, 0.0, rows + 1).astype(BF16)
        for q in range(rows):
            at = jnp.broadcast_to(one[q:q + 1, :], (lev, blk))
            if q:
                below = jnp.broadcast_to(one[q - 1:q, :], (lev, blk))
                x[q * lev:(q + 1) * lev, 0:blk] = u_hi * at + v_hi * below
                x[q * lev:(q + 1) * lev, blk:] = u_lo * at + v_lo * below
            else:
                x[0:lev, 0:blk] = u_hi * at
                x[0:lev, blk:] = u_lo * at
        acc[...] += lax.dot_general(x[...], jnp.concatenate([right, right], 1), (((1,), (1,)), ((), ())), preferred_element_type=F32)
        return 0
    lax.fori_loop(0, nb, step, 0)
    for r in range(rows):
        a = acc[r * lev:(r + 1) * lev, :]
        out_ref[r] = a[:, 0:cols] + a[:, cols:]


def scatter(cells, weights, back, rows, cols):
    n2, lev, _ = back.shape
    nb = n2 // 2
    return pl.pallas_call(functools.partial(scatter_kernel, rows, lev, cols, nb),
        out_shape=jax.ShapeDtypeStruct((rows, lev, cols), F32),
        in_specs=[pl.BlockSpec(memory_space=VMEM)] * 3,
        out_specs=pl.BlockSpec(memory_space=VMEM), name="scatter",
        scratch_shapes=[VMEM((rows * lev, 512), BF16), VMEM((rows * lev, 256), F32)],
        compiler_params=params(20),
    )(cells, weights, back)


def group_start(g, levels):
    start, last = LANES8 * g, levels - LANES8
    return min(start, last) if isinstance(g, int) else jnp.minimum(start, last)


def params(megabytes):
    return pltpu.CompilerParams(vmem_limit_bytes=megabytes * 2**20)


def lanes_of(g):
    return pl.ds(pl.multiple_of(LANES8 * g, LANES8), LANES8)


def obs_kernel(levels, value_ref, precision_ref, live_ref, out_ref):
    def step(p, _):
        here = pl.ds(pl.multiple_of(p * 128, 128), 128)
        live = live_ref[0:1, here] > 0
        out_ref[p, 0:levels, :] = value_ref[:, here]
        out_ref[p, levels:2 * levels, :] = jnp.where(live, precision_ref[:, here], 0.0)
        return 0
    lax.fori_loop(0, out_ref.shape[0], step, 0)


def obs_blocks(value, precision, live):
    levels, slots = value.shape
    return pl.pallas_call(functools.partial(obs_kernel, levels), name="obs_blocks",
        out_shape=jax.ShapeDtypeStruct((slots // 128, -(-2 * levels // LANES8) * LANES8, 128), F32),
        in_specs=[WHOLE] * 3, out_specs=WHOLE, compiler_params=params(12))(value, precision, live)


def turn(x, shift):
    shift = shift % 128
    return pltpu.roll(x, shift, x.ndim - 1) if shift else x


def place(rows):
    lane = lax.broadcasted_iota(jnp.int32, (rows, LANES8, 128), 2)
    return lane, lane % (4 * STEPS)


def slabs_of(groups):
    slabs = -(-groups // 8)
    return slabs, -(-groups // slabs)


def pack_strip(load, groups, rows, margin):
    lane, _ = place(rows)
    width = 4 * margin
    west = east = jnp.zeros((rows, LANES8, 128), F32)
    for g in range(groups):
        x = load(g)
        here = (lane >= width * g) & (lane < width * (g + 1))
        west = jnp.where(here, turn(x, width * g + margin), west)
        east = jnp.where(here, turn(x, width * g + 2 * margin), east)
    return west, east


def pack_sends(strips, rows, margin):
    _, at = place(rows)
    to_east = to_west = jnp.zeros((rows, LANES8, 128), F32)
    for f, (west, east) in enumerate(strips):
        here = (at >= margin * f) & (at < margin * (f + 1))
        to_east = jnp.where(here, turn(east, margin * f - margin), to_east)
        to_west = jnp.where(here, turn(west, margin * f - margin), to_west)
    return to_east, to_west


def complete(f, west, east, from_west, from_east, rows, margin):
    _, at = place(rows)
    west = jnp.where(at < margin, turn(from_west, -margin * f), west)
    east = jnp.where(at >= 2 * margin, turn(from_east, 2 * margin - margin * f), east)
    return west, east


def slab_load(ref, at, count, slab, per):
    return lambda g: ref[pl.ds(at, count), LANES8 * (slab * per + g):LANES8 * (slab * per + g + 1), :]


def stage_kernel(groups, levels, margin, control_ref, east_ref, north_ref, mask_ref, *outs):
    cols = control_ref.shape[2]
    refs = [ref.reshape(levels * LANES8, cols) for ref in (control_ref, east_ref, north_ref, mask_ref)]
    block, last = pl.program_id(0), pl.num_programs(0) - 1
    field_refs, (top_ref, bottom_ref, strip_ref) = outs[:4], outs[4:]
    def step(g, _):
        start = group_start(g, levels)
        for r in range(LANES8):
            where = pl.ds(start * LANES8 + r, LANES8, stride=LANES8)
            control, east, north, mask = (ref[where, :] for ref in refs)
            mask = mask.astype(F32)
            for ref, value in zip(field_refs, (mask * control, mask, east, north)):
                ref[r, lanes_of(g), :] = value
        return 0
    lax.fori_loop(0, groups, step, 0)
    slabs, per = slabs_of(groups)
    count = 2
    def pack(i, _):
        at = count * i
        for slab in range(slabs):
            for f in range(4):
                west, east = pack_strip(slab_load(field_refs[f], at, count, slab, per), min(per, groups - slab * per), count, margin)
                strip_ref[f, 0, slab, pl.ds(at, count)] = west
                strip_ref[f, 1, slab, pl.ds(at, count)] = east
        return 0
    lax.fori_loop(0, LANES8 // count, pack, 0)
    @pl.when(block == 0)
    def _():
        for f in range(4):
            bottom_ref[f * margin:(f + 1) * margin] = field_refs[f][0:margin]
    @pl.when(block == last)
    def _():
        for f in range(4):
            top_ref[f * margin:(f + 1) * margin] = field_refs[f][LANES8 - margin:LANES8]


def stage(groups, margin, natural):
    levels, rows, cols = natural[0].shape
    depth = LANES8 * groups
    slabs, _ = slabs_of(groups)
    natural = [pltpu.with_memory_space_constraint(x, pltpu.HBM) for x in natural]
    return pl.pallas_call(functools.partial(stage_kernel, groups, levels, margin),
        grid=(rows // LANES8,), name="stage",
        out_shape=[jax.ShapeDtypeStruct((rows, depth, cols), F32)] * 4 + [jax.ShapeDtypeStruct((4 * margin, depth, cols), F32)] * 2
        + [jax.ShapeDtypeStruct((4, 2, slabs, rows, LANES8, 128), F32)],
        in_specs=[pl.BlockSpec((levels, LANES8, cols), lambda i: (0, i, 0))] * 4,
        out_specs=[pl.BlockSpec((LANES8, depth, cols), lambda i: (i, 0, 0))] * 4 + [pl.BlockSpec((4 * margin, depth, cols), lambda i: (0, 0, 0))] * 2
        + [pl.BlockSpec((4, 2, slabs, LANES8, LANES8, 128), lambda i: (0, 0, 0, i, 0, 0))],
        compiler_params=params(16))(*natural)


def sends_kernel(groups, levels, margin, control_ref, east_ref, north_ref, mask_ref, to_east, to_west):
    cols = control_ref.shape[2]
    refs = [ref.reshape(levels * LANES8, cols) for ref in (control_ref, east_ref, north_ref, mask_ref)]
    slabs, per = slabs_of(groups)
    quad = lax.broadcasted_iota(jnp.int32, (LANES8, 128), 1) // margin
    for r in range(LANES8):
        for slab in range(slabs):
            east_out = west_out = jnp.zeros((LANES8, 128), F32)
            for g in range(min(per, groups - slab * per)):
                where = pl.ds(group_start(slab * per + g, levels) * LANES8 + r, LANES8, stride=LANES8)
                control, east, north, mask = (ref[where, :] for ref in refs)
                mask = mask.astype(F32)
                for f, x in enumerate((mask * control, mask, east, north)):
                    here = quad == 4 * g + f
                    east_out = jnp.where(here, turn(x, margin * (4 * g + f + 1) - cols), east_out)
                    west_out = jnp.where(here, turn(x, margin * (4 * g + f)), west_out)
            to_east[slab, r] = east_out
            to_west[slab, r] = west_out


def lon_sends(groups, margin, natural):
    levels, rows, cols = natural[0].shape
    slabs, _ = slabs_of(groups)
    natural = [pltpu.with_memory_space_constraint(x, pltpu.HBM) for x in natural]
    return pl.pallas_call(functools.partial(sends_kernel, groups, levels, margin), grid=(rows // LANES8,), name="lon_sends",
        out_shape=[jax.ShapeDtypeStruct((slabs, rows, LANES8, 128), F32)] * 2,
        in_specs=[pl.BlockSpec((levels, LANES8, cols), lambda i: (0, i, 0))] * 4,
        out_specs=[pl.BlockSpec((slabs, LANES8, LANES8, 128), lambda i: (0, i, 0, 0))] * 2,
        compiler_params=params(16))(*natural)


def rim_kernel(groups, margin, south_in, north_in, strip_ref):
    slabs, per = slabs_of(groups)
    for slab in range(slabs):
        for f in range(4):
            for end, ref in enumerate((south_in, north_in)):
                west, east = pack_strip(slab_load(ref, f * margin, margin, slab, per), min(per, groups - slab * per), margin, margin)
                strip_ref[f, 0, slab, end * margin:(end + 1) * margin] = west
                strip_ref[f, 1, slab, end * margin:(end + 1) * margin] = east


def strip_rims(groups, margin, south_in, north_in):
    slabs, _ = slabs_of(groups)
    return pl.pallas_call(functools.partial(rim_kernel, groups, margin),
        out_shape=jax.ShapeDtypeStruct((4, 2, slabs, 2 * margin, LANES8, 128), F32),
        in_specs=[WHOLE] * 2, out_specs=WHOLE, name="strip_rims", compiler_params=params(12))(south_in, north_in)


def faces_kernel(groups, rows, margin, mask_ref, east_ref, north_ref, south_in, north_in, e_out, n_out, mask):
    tall = rows + 2 * margin
    def step(g, _):
        put = lanes_of(g)
        mask[0:margin] = south_in[margin:2 * margin, put, :]
        mask[margin:margin + rows] = mask_ref[:, put, :]
        mask[margin + rows:tall] = north_in[margin:2 * margin, put, :]
        pieces = [(0, margin, south_in, 0), (margin + rows, margin, north_in, 0)] + [(margin + i, LANES8, None, i) for i in range(0, rows, LANES8)]
        for at, count, halo, i in pieces:
            if halo is None:
                east, north = east_ref[i:i + count, put, :], north_ref[i:i + count, put, :]
            else:
                east, north = halo[2 * margin:3 * margin, put, :], halo[3 * margin:4 * margin, put, :]
            own = mask[at:at + count]
            e_out[at:at + count, put, :] = east * own * turn(own, -1)
            n_out[at:at + count, put, :] = north * own * mask[at + 1:at + count + 1]
        return 0
    mask[tall] = jnp.zeros((LANES8, 128), F32)
    lax.fori_loop(0, groups, step, 0)


def faces(groups, rows, margin, fields, south_in, north_in):
    tall = rows + 2 * margin
    return pl.pallas_call(functools.partial(faces_kernel, groups, rows, margin),
        out_shape=[jax.ShapeDtypeStruct((tall, LANES8 * groups, 128), F32)] * 2,
        in_specs=[WHOLE] * 5, out_specs=[WHOLE] * 2, name="faces", scratch_shapes=[VMEM((tall + 1, LANES8, 128), F32)],
        compiler_params=params(12))(*fields[1:], south_in, north_in)


def sweep(source, east, north, write, low, high):
    for at in range(low, high, LANES8):
        end = min(at + LANES8, high)
        u = source(at - 1, end + 1)
        rise = north(at - 1, end) * (u[1:] - u[:-1])
        u = u[1:-1]
        run = east(at, end) * (turn(u, -1) - u)
        write(at, end, u + ((run - turn(run, 1)) + (rise[1:] - rise[:-1])))


def reader(ref, *lead):
    return lambda at, end: ref[(*lead, slice(at, end))]


def writer(ref, *lead):
    def write(at, end, value):
        ref[(*lead, slice(at, end))] = value
    return write


def all_sweeps(tall, margin, states, east, north, write):
    for k in range(margin):
        now, later = states[k % 2], states[(k + 1) % 2]
        sweep(reader(now), east, north, writer(later) if k + 1 < margin else write, k + 1, tall - 1 - k)


def strip_sweeps(rows, margin, strip_refs, faces_ref, rim):
    tall = rows + 2 * margin
    last = strip_refs[margin % 2]
    def step(slab, _):
        for side in range(2):
            states = [ref.at[side, slab] for ref in strip_refs]
            all_sweeps(tall, margin, states, reader(faces_ref, side, 0, slab), reader(faces_ref, side, 1, slab), writer(states[margin % 2]))
        for i in range(0, rows, LANES8):
            _, at = place(LANES8)
            here = slice(i + margin, i + margin + LANES8)
            rim[slab, i:i + LANES8] = jnp.where(at < margin, turn(last[1, slab, here], -margin), last[0, slab, here])
        return 0
    lax.fori_loop(0, rim.shape[0], step, 0)


def put_rim(x, g, groups, margin, rim):
    _, per = slabs_of(groups)
    slab = g // per
    lane = lax.broadcasted_iota(jnp.int32, x.shape, x.ndim - 1)
    edge = rim(slab)
    shift = 128 - margin - 4 * margin * (g - slab * per)
    edge = turn(edge, shift) if isinstance(shift, int) else pltpu.roll(edge, shift, edge.ndim - 1)
    return jnp.where((lane < margin) | (lane >= 128 - margin), edge, x)


def tiles_kernel(groups, rows, margin, u_ref, south_in, north_in, e_ref, n_ref, out_ref, state_a, state_b):
    tall = rows + 2 * margin
    def step(g, _):
        put = lanes_of(g)
        fill(state_a, put, south_in, u_ref, north_in, margin, 0)
        def write(at, end, value):
            out_ref[at - margin:end - margin, put, :] = value
        all_sweeps(tall, margin, (state_a, state_b), lambda a, b: e_ref[a:b, put, :], lambda a, b: n_ref[a:b, put, :], write)
        return 0
    lax.fori_loop(0, groups, step, 0)


def tiles(groups, rows, margin, u, south_in, north_in, e, n):
    tall = rows + 2 * margin
    size = rows * LANES8 * groups * 128
    return pl.pallas_call(functools.partial(tiles_kernel, groups, rows, margin),
        out_shape=jax.ShapeDtypeStruct((rows, LANES8 * groups, 128), F32),
        in_specs=[WHOLE] * 5, out_specs=WHOLE, name="tiles", scratch_shapes=[VMEM((tall, LANES8, 128), F32)] * 2,
        cost_estimate=pl.CostEstimate(flops=40 * size, bytes_accessed=20 * size, transcendentals=0),
        compiler_params=params(16))(u, south_in, north_in, e, n)


def fill(state, put, low, middle, high, margin, offset):
    rows = middle.shape[0]
    state[0:margin] = low[offset:offset + margin, put, :]
    state[margin:margin + rows] = middle[:, put, :]
    state[margin + rows:2 * margin + rows] = high[offset:offset + margin, put, :]


def forward_kernel(rows, margin, strip_ref, from_west, from_east, rims_ref, south_corners, north_corners, rim, faces_ref, strip_a, strip_b, mask):
    tall = rows + 2 * margin
    def join(slab, _):
        for side in range(2):
            mask[side, tall] = jnp.zeros((LANES8, 128), F32)
        pieces = [(0, margin, rims_ref, 0, south_corners.at[0, slab], south_corners.at[1, slab], 0),
                  (margin + rows, margin, rims_ref, margin, north_corners.at[0, slab], north_corners.at[1, slab], 0)]
        pieces += [(margin + i, LANES8, strip_ref, i, from_west.at[slab], from_east.at[slab], i) for i in range(0, rows, LANES8)]
        for at, count, own_ref, own_at, west_ref, east_ref, in_at in pieces:
            here, there, source = slice(at, at + count), slice(own_at, own_at + count), slice(in_at, in_at + count)
            for f in range(4):
                pair = complete(f, own_ref[f, 0, slab, there], own_ref[f, 1, slab, there], west_ref[source], east_ref[source], count, margin)
                for side, value in enumerate(pair):
                    if f == 0:
                        strip_a[side, slab, here] = value
                    elif f == 1:
                        mask[side, here] = value
                    else:
                        faces_ref[side, f - 2, slab, here] = value
        for at in range(0, tall, LANES8):
            here = slice(at, at + LANES8)
            for side in range(2):
                own = mask[side, here]
                faces_ref[side, 0, slab, here] = faces_ref[side, 0, slab, here] * own * turn(own, -1)
                faces_ref[side, 1, slab, here] = faces_ref[side, 1, slab, here] * own * mask[side, at + 1:at + 1 + LANES8]
        return 0
    lax.fori_loop(0, rim.shape[0], join, 0)
    strip_sweeps(rows, margin, (strip_a, strip_b), faces_ref, rim)


def forward_strips(groups, rows, margin, *args):
    tall = rows + 2 * margin
    slabs, _ = slabs_of(groups)
    return pl.pallas_call(functools.partial(forward_kernel, rows, margin),
        out_shape=[jax.ShapeDtypeStruct((slabs, rows, LANES8, 128), F32), jax.ShapeDtypeStruct((2, 2, slabs, tall, LANES8, 128), F32)],
        in_specs=[WHOLE] * 6, out_specs=[WHOLE] * 2, name="forward_strips",
        scratch_shapes=[VMEM((2, slabs, tall, LANES8, 128), F32)] * 2 + [VMEM((2, tall + 1, LANES8, 128), F32)],
        compiler_params=params(16))(*args)


def strip_adjoint_kernel(groups, rows, margin, adjoint_ref, south_in, north_in, strip_ref, to_east, to_west):
    quarter = (rows + 2 * margin) // 4
    slabs, per = slabs_of(groups)
    def build(ref, i, at):
        for slab in range(slabs):
            west, east = pack_strip(slab_load(ref, i, 2, slab, per), min(per, groups - slab * per), 2, margin)
            strip_ref[0, slab, pl.ds(at, 2)] = west
            strip_ref[1, slab, pl.ds(at, 2)] = east
    for i in range(0, margin, 2):
        build(south_in, i, i)
        build(north_in, i, i + margin + rows)
    def inside(i, _):
        build(adjoint_ref, 2 * i, 2 * i + margin)
        return 0
    lax.fori_loop(0, rows // 2, inside, 0)
    for slab in range(slabs):
        for at in range(0, quarter, 2):
            here = [slice(at + q * quarter, at + q * quarter + 2) for q in range(4)]
            sends = pack_sends([(strip_ref[0, slab, s], strip_ref[1, slab, s]) for s in here], 2, margin)
            to_east[slab, at:at + 2], to_west[slab, at:at + 2] = sends


def strip_adjoint(groups, rows, margin, adjoint, south_in, north_in):
    tall = rows + 2 * margin
    slabs, _ = slabs_of(groups)
    return pl.pallas_call(functools.partial(strip_adjoint_kernel, groups, rows, margin),
        out_shape=[jax.ShapeDtypeStruct((2, slabs, tall, LANES8, 128), F32)] + [jax.ShapeDtypeStruct((slabs, tall // 4, LANES8, 128), F32)] * 2,
        in_specs=[WHOLE] * 3, out_specs=[WHOLE] * 3, name="strip_adjoint", compiler_params=params(12))(adjoint, south_in, north_in)


def finish_kernel(groups, levels, rows, margin, tiles_ref, strip_ref, from_west, from_east, faces_ref, u_ref, mask_ref, out_ref, strip_a, strip_b, rim):
    quarter = (rows + 2 * margin) // 4
    for slab in range(rim.shape[0]):
        for at in range(0, quarter, 2):
            for q in range(4):
                here = slice(at + q * quarter, at + q * quarter + 2)
                pair = complete(q, strip_ref[0, slab, here], strip_ref[1, slab, here], from_west[slab, at:at + 2], from_east[slab, at:at + 2], 2, margin)
                for side in range(2):
                    strip_a[side, slab, here] = pair[side]
    strip_sweeps(rows, margin, (strip_a, strip_b), faces_ref, rim)
    def step(g, _):
        put = lanes_of(g)
        start = group_start(g, levels)
        for at in range(0, rows, LANES8):
            here = slice(at, at + LANES8)
            value = put_rim(tiles_ref[here, put, :], g, groups, margin, lambda slab: rim[slab, here])
            value = u_ref[here, put, :] + mask_ref[here, put, :] * value
            for r in range(LANES8):
                out_ref[pl.ds(start * rows + at + r, LANES8, stride=rows), :] = value[r]
        return 0
    lax.fori_loop(0, groups, step, 0)


def finish(groups, levels, rows, margin, *args):
    tall = rows + 2 * margin
    slabs, _ = slabs_of(groups)
    return pl.pallas_call(functools.partial(finish_kernel, groups, levels, rows, margin),
        out_shape=jax.ShapeDtypeStruct((levels * rows, 128), F32),
        in_specs=[WHOLE] * 7, out_specs=WHOLE, name="finish",
        scratch_shapes=[VMEM((2, slabs, tall, LANES8, 128), F32)] * 2 + [VMEM((slabs, rows, LANES8, 128), F32)],
        compiler_params=params(20))(*args)


def departures_kernel(groups, levels, equivalent_ref, obs_ref, out_ref, back_ref):
    def step(p, _):
        for g in range(groups):
            start = group_start(g, levels)
            here = slice(LANES8 * g, LANES8 * (g + 1))
            gap = obs_ref[p, levels + start:levels + start + LANES8, :] * (equivalent_ref[p, here, :] - obs_ref[p, start:start + LANES8, :])
            back_ref[p, here, :] = gap
            out_ref[p, start:start + LANES8, :] = gap
        return 0
    lax.fori_loop(0, out_ref.shape[0], step, 0, unroll=2)


def departures_of(groups, levels, equivalent, obs):
    return pl.pallas_call(functools.partial(departures_kernel, groups, levels),
        out_shape=[jax.ShapeDtypeStruct((equivalent.shape[0], levels, 128), F32), jax.ShapeDtypeStruct(equivalent.shape, F32)],
        in_specs=[WHOLE] * 2, out_specs=[WHOLE] * 2, name="departures", compiler_params=params(16))(equivalent, obs)


def place_kernel(part_ref, out_ref):
    def step(p, _):
        out_ref[:, pl.ds(pl.multiple_of(p * 128, 128), 128)] = part_ref[p]
        return 0
    lax.fori_loop(0, part_ref.shape[0], step, 0, unroll=2)


def place_departures(part):
    blocks, levels, width = part.shape
    return pl.pallas_call(place_kernel, name="place_departures",
        out_shape=jax.ShapeDtypeStruct((levels, blocks * width), F32),
        in_specs=[WHOLE], out_specs=WHOLE, compiler_params=params(12))(part)


def exchange(values, share):
    blocks, levels, width = values.shape
    if share > 1:
        values = values.reshape(blocks, levels, share, -1).transpose(0, 2, 1, 3)
    values = values.reshape(blocks * share, levels, width // share)
    values = lax.all_to_all(values, ("gx", "gy"), 0, 0, tiled=True)
    if share > 1:
        values = values.reshape(blocks, share, levels, -1).transpose(0, 2, 1, 3)
    return values.reshape(blocks, levels, width)


def pass_around(axis, forth, back):
    size = lax.axis_size(axis)
    up = [(i, (i + 1) % size) for i in range(size)]
    return lax.ppermute(forth, axis, up), lax.ppermute(back, axis, [(j, i) for i, j in up])


def swap_edges(axis, forth, back):
    size, odd = lax.axis_size(axis), lax.axis_index(axis) % 2 == 1
    rounds = [[pair for i in range(first, size - 1, 2) for pair in ((i, i + 1), (i + 1, i))] for first in range(2)]
    inner = lax.ppermute(jnp.where(odd, back, forth), axis, rounds[0])
    outer = lax.ppermute(jnp.where(odd, forth, back), axis, rounds[1])
    return jnp.where(odd, inner, outer), jnp.where(odd, outer, inner)


def body(
    control,
    east_coeff,
    north_coeff,
    ocean_mask,
    corner_cells,
    corner_weights,
    obs_value,
    obs_precision,
    slot_counts,
):
    levels, rows, cols = control.shape
    slots = corner_cells.shape[1]
    capacity = slots // lax.axis_size(("gx", "gy"))
    share = 128 // capacity
    margin = STEPS
    live = (slot_counts[0][:, None] > jnp.arange(capacity)[None, :]).astype(jnp.int32).reshape(1, slots)
    groups = -(-levels // 16) * 2
    natural = (control, east_coeff, north_coeff, ocean_mask)
    to_east, to_west = lon_sends(groups, margin, natural)
    from_west, from_east = pass_around("gx", to_east, to_west)
    obs = obs_blocks(obs_value, obs_precision, live)
    obs, *_ = lax.optimization_barrier((obs, to_east, to_west))
    obs = exchange(obs, share)
    *fields, top, bottom, strip = stage(groups, margin, natural)
    south_in, north_in = swap_edges("gy", top, bottom)
    corners = jnp.stack([from_west, from_east])
    south_corners, north_corners = swap_edges("gy", corners[:, :, rows - margin:], corners[:, :, :margin])
    rims = strip_rims(groups, margin, south_in, north_in)
    e, n = faces(groups, rows, margin, fields, south_in, north_in)
    background = tiles(groups, rows, margin, fields[0], south_in, north_in, e, n)
    rim, strip_faces = forward_strips(groups, rows, margin, strip, from_west, from_east, rims, south_corners, north_corners)
    equivalent = gather(corner_cells, corner_weights, background, rim, slots, margin)
    out, back = departures_of(groups, levels, equivalent, obs)
    sent = exchange(out, share)
    adjoint = scatter(corner_cells, corner_weights, back, rows, cols)
    south_in, north_in = swap_edges("gy", adjoint[rows - margin:], adjoint[:margin])
    strip, to_east, to_west = strip_adjoint(groups, rows, margin, adjoint, south_in, north_in)
    from_west, from_east = pass_around("gx", to_east, to_west)
    departures = place_departures(sent)
    swept = tiles(groups, rows, margin, adjoint, south_in, north_in, e, n)
    gradient = finish(groups, levels, rows, margin, swept, strip, from_west, from_east, strip_faces, fields[0], fields[1])
    return gradient.reshape(levels, rows, cols), departures


def solution(mesh):
    return jax.shard_map(
        body,
        mesh=mesh,
        in_specs=(
            P(None, "gy", "gx"),
            P(None, "gy", "gx"),
            P(None, "gy", "gx"),
            P(None, "gy", "gx"),
            P(None, ("gx", "gy")),
            P(None, ("gx", "gy")),
            P(None, ("gx", "gy")),
            P(None, ("gx", "gy")),
            P(("gx", "gy"), None),
        ),
        out_specs=(P(None, "gy", "gx"), P(None, ("gx", "gy"))),
        check_vma=False,
    )
```

```python
import functools

import jax
import jax.numpy as jnp
from jax import lax
from jax.experimental import pallas as pl
from jax.experimental.pallas import tpu as pltpu
from jax.sharding import PartitionSpec as P


F32, BF16 = jnp.float32, jnp.bfloat16
VMEM = pltpu.VMEM
STEPS = 4
LANES8 = 8
WHOLE = pl.BlockSpec(memory_space=pltpu.VMEM)


def split2(x):
    hi = x.astype(BF16)
    lo = (x - hi.astype(F32)).astype(BF16)
    return hi, lo


def hats(cells_ref, weights_ref, j0, n, cols):
    c = cells_ref[0:1, pl.ds(j0, n)]
    w = weights_ref[:, pl.ds(j0, n)]
    r = c // cols
    s = c - r * cols
    east, west = w[1:2] + w[3:4], w[0:1] + w[2:3]
    north, south = w[2:3] + w[3:4], w[0:1] + w[1:2]
    return r, s, east, west, north, south


def hat(index, low, high, size):
    at = lax.broadcasted_iota(jnp.int32, (size, index.shape[1]), 0) - index
    return jnp.where(at == 0, low, jnp.where(at == 1, high, 0.0))


def gather_kernel(rows, lev, cols, nb, margin, cells_ref, weights_ref, bg_ref, rim_ref, out_ref, bb, t0, t1, rr0, rr1):
    for r in range(rows):
        parts = [put_rim(bg_ref[r, 8 * g:8 * g + 8, :], g, lev // 8, margin, lambda slab: rim_ref[slab, r]) for g in range(lev // 8)]
        hi, lo = split2(jnp.concatenate(parts, 0))
        bb[r * lev:(r + 1) * lev, 0:cols] = hi
        bb[r * lev:(r + 1) * lev, cols:2 * cols] = lo
    blk = 256
    def multiply(jb, t, rr):
        r, s, east, west, north, south = hats(cells_ref, weights_ref, pl.multiple_of(jb * blk, blk), blk, cols)
        rr[...] = hat(r, south, north, rows)
        hi, lo = split2(hat(s, west, east, cols))
        left = bb[...]
        t[...] = (jnp.dot(left, jnp.concatenate([hi, hi], 0), preferred_element_type=F32)
                  + jnp.dot(left, jnp.concatenate([lo, lo], 0), preferred_element_type=F32))
    def reduce(jb, t, rr):
        acc = jnp.zeros((lev, blk), F32)
        for r in range(rows):
            acc = acc + t[r * lev:(r + 1) * lev, :] * rr[r:r + 1, :]
        out_ref[2 * jb] = acc[:, 0:128]
        out_ref[2 * jb + 1] = acc[:, 128:256]
    def step(i, _):
        multiply(2 * i, t0, rr0)
        multiply(2 * i + 1, t1, rr1)
        reduce(2 * i, t0, rr0)
        reduce(2 * i + 1, t1, rr1)
        return 0
    lax.fori_loop(0, nb // 2, step, 0)


def gather(cells, weights, bg, rim, slots, margin):
    rows, lev, cols = bg.shape
    nb = slots // 256
    return pl.pallas_call(functools.partial(gather_kernel, rows, lev, cols, nb, margin),
        out_shape=jax.ShapeDtypeStruct((2 * nb, lev, 128), F32),
        in_specs=[pl.BlockSpec(memory_space=VMEM)] * 4,
        out_specs=pl.BlockSpec(memory_space=VMEM), name="gather",
        scratch_shapes=[VMEM((rows * lev, 2 * cols), BF16), VMEM((rows * lev, 256), F32), VMEM((rows * lev, 256), F32), VMEM((rows, 256), F32), VMEM((rows, 256), F32)],
        compiler_params=params(20),
    )(cells, weights, bg, rim)


def scatter_kernel(rows, lev, cols, nb, cells_ref, weights_ref, back_ref, out_ref, x, acc):
    blk = 256
    acc[...] = jnp.zeros_like(acc)
    def step(jb, _):
        r, s, east, west, north, south = hats(cells_ref, weights_ref, pl.multiple_of(jb * blk, blk), blk, cols)
        hi, lo = split2(hat(s, west, east, cols))
        right = jnp.concatenate([hi, lo], 0)
        back = jnp.concatenate([back_ref[2 * jb], back_ref[2 * jb + 1]], 1)
        u_hi, u_lo = split2(back * south)
        v_hi, v_lo = split2(back * north)
        one = hat(r, 1.0, 0.0, rows + 1).astype(BF16)
        for q in range(rows):
            at = jnp.broadcast_to(one[q:q + 1, :], (lev, blk))
            if q:
                below = jnp.broadcast_to(one[q - 1:q, :], (lev, blk))
                x[q * lev:(q + 1) * lev, 0:blk] = u_hi * at + v_hi * below
                x[q * lev:(q + 1) * lev, blk:] = u_lo * at + v_lo * below
            else:
                x[0:lev, 0:blk] = u_hi * at
                x[0:lev, blk:] = u_lo * at
        acc[...] += lax.dot_general(x[...], jnp.concatenate([right, right], 1), (((1,), (1,)), ((), ())), preferred_element_type=F32)
        return 0
    lax.fori_loop(0, nb, step, 0)
    for r in range(rows):
        a = acc[r * lev:(r + 1) * lev, :]
        out_ref[r] = a[:, 0:cols] + a[:, cols:]


def scatter(cells, weights, back, rows, cols):
    n2, lev, _ = back.shape
    nb = n2 // 2
    return pl.pallas_call(functools.partial(scatter_kernel, rows, lev, cols, nb),
        out_shape=jax.ShapeDtypeStruct((rows, lev, cols), F32),
        in_specs=[pl.BlockSpec(memory_space=VMEM)] * 3,
        out_specs=pl.BlockSpec(memory_space=VMEM), name="scatter",
        scratch_shapes=[VMEM((rows * lev, 512), BF16), VMEM((rows * lev, 256), F32)],
        compiler_params=params(20),
    )(cells, weights, back)


def group_start(g, levels):
    start, last = LANES8 * g, levels - LANES8
    return min(start, last) if isinstance(g, int) else jnp.minimum(start, last)


def params(megabytes):
    return pltpu.CompilerParams(vmem_limit_bytes=megabytes * 2**20)


def lanes_of(g):
    return pl.ds(pl.multiple_of(LANES8 * g, LANES8), LANES8)


def obs_kernel(levels, value_ref, precision_ref, live_ref, out_ref):
    def step(p, _):
        here = pl.ds(pl.multiple_of(p * 128, 128), 128)
        live = live_ref[0:1, here] > 0
        out_ref[p, 0:levels, :] = value_ref[:, here]
        out_ref[p, levels:2 * levels, :] = jnp.where(live, precision_ref[:, here], 0.0)
        return 0
    lax.fori_loop(0, out_ref.shape[0], step, 0)


def obs_blocks(value, precision, live):
    levels, slots = value.shape
    return pl.pallas_call(functools.partial(obs_kernel, levels), name="obs_blocks",
        out_shape=jax.ShapeDtypeStruct((slots // 128, -(-2 * levels // LANES8) * LANES8, 128), F32),
        in_specs=[WHOLE] * 3, out_specs=WHOLE, compiler_params=params(12))(value, precision, live)


def turn(x, shift):
    shift = shift % 128
    return pltpu.roll(x, shift, x.ndim - 1) if shift else x


def place(rows):
    lane = lax.broadcasted_iota(jnp.int32, (rows, LANES8, 128), 2)
    return lane, lane % (4 * STEPS)


def slabs_of(groups):
    slabs = -(-groups // 8)
    return slabs, -(-groups // slabs)


def pack_strip(load, groups, rows, margin):
    lane, _ = place(rows)
    width = 4 * margin
    west = east = jnp.zeros((rows, LANES8, 128), F32)
    for g in range(groups):
        x = load(g)
        here = (lane >= width * g) & (lane < width * (g + 1))
        west = jnp.where(here, turn(x, width * g + margin), west)
        east = jnp.where(here, turn(x, width * g + 2 * margin), east)
    return west, east


def pack_sends(strips, rows, margin):
    _, at = place(rows)
    to_east = to_west = jnp.zeros((rows, LANES8, 128), F32)
    for f, (west, east) in enumerate(strips):
        here = (at >= margin * f) & (at < margin * (f + 1))
        to_east = jnp.where(here, turn(east, margin * f - margin), to_east)
        to_west = jnp.where(here, turn(west, margin * f - margin), to_west)
    return to_east, to_west


def complete(f, west, east, from_west, from_east, rows, margin):
    _, at = place(rows)
    west = jnp.where(at < margin, turn(from_west, -margin * f), west)
    east = jnp.where(at >= 2 * margin, turn(from_east, 2 * margin - margin * f), east)
    return west, east


def slab_load(ref, at, count, slab, per):
    return lambda g: ref[pl.ds(at, count), LANES8 * (slab * per + g):LANES8 * (slab * per + g + 1), :]


def stage_kernel(groups, levels, margin, control_ref, east_ref, north_ref, mask_ref, *outs):
    cols = control_ref.shape[2]
    refs = [ref.reshape(levels * LANES8, cols) for ref in (control_ref, east_ref, north_ref, mask_ref)]
    *field_refs, strip_ref = outs
    def step(g, _):
        start = group_start(g, levels)
        for r in range(LANES8):
            where = pl.ds(start * LANES8 + r, LANES8, stride=LANES8)
            control, east, north, mask = (ref[where, :] for ref in refs)
            mask = mask.astype(F32)
            for ref, value in zip(field_refs, (mask * control, mask, east, north)):
                ref[r, lanes_of(g), :] = value
        return 0
    lax.fori_loop(0, groups, step, 0)
    slabs, per = slabs_of(groups)
    count = 2
    def pack(i, _):
        at = count * i
        for slab in range(slabs):
            for f in range(4):
                west, east = pack_strip(slab_load(field_refs[f], at, count, slab, per), min(per, groups - slab * per), count, margin)
                strip_ref[f, 0, slab, pl.ds(at, count)] = west
                strip_ref[f, 1, slab, pl.ds(at, count)] = east
        return 0
    lax.fori_loop(0, LANES8 // count, pack, 0)


def stage(groups, margin, natural):
    levels, rows, cols = natural[0].shape
    depth = LANES8 * groups
    slabs, _ = slabs_of(groups)
    natural = [pltpu.with_memory_space_constraint(x, pltpu.HBM) for x in natural]
    return pl.pallas_call(functools.partial(stage_kernel, groups, levels, margin),
        grid=(rows // LANES8,), name="stage",
        out_shape=[jax.ShapeDtypeStruct((rows, depth, cols), F32)] * 4
        + [jax.ShapeDtypeStruct((4, 2, slabs, rows, LANES8, 128), F32)],
        in_specs=[pl.BlockSpec((levels, LANES8, cols), lambda i: (0, i, 0))] * 4,
        out_specs=[pl.BlockSpec((LANES8, depth, cols), lambda i: (i, 0, 0))] * 4
        + [pl.BlockSpec((4, 2, slabs, LANES8, LANES8, 128), lambda i: (0, 0, 0, i, 0, 0))],
        compiler_params=params(16))(*natural)


def sends_kernel(groups, levels, margin, odd_ref, control_ref, east_ref, north_ref, mask_ref, to_east, to_west, inner_ref, outer_ref):
    cols = control_ref.shape[2]
    refs = [ref.reshape(levels * LANES8, cols) for ref in (control_ref, east_ref, north_ref, mask_ref)]
    slabs, per = slabs_of(groups)
    quad = lax.broadcasted_iota(jnp.int32, (LANES8, 128), 1) // margin
    for r in range(LANES8):
        for slab in range(slabs):
            east_out = west_out = jnp.zeros((LANES8, 128), F32)
            for g in range(min(per, groups - slab * per)):
                where = pl.ds(group_start(slab * per + g, levels) * LANES8 + r, LANES8, stride=LANES8)
                control, east, north, mask = (ref[where, :] for ref in refs)
                mask = mask.astype(F32)
                for f, x in enumerate((mask * control, mask, east, north)):
                    here = quad == 4 * g + f
                    east_out = jnp.where(here, turn(x, margin * (4 * g + f + 1) - cols), east_out)
                    west_out = jnp.where(here, turn(x, margin * (4 * g + f)), west_out)
            to_east[slab, r] = east_out
            to_west[slab, r] = west_out
    block, last = pl.program_id(0), pl.num_programs(0) - 1
    odd = odd_ref[0]
    def edge(out_ref, first):
        def step(g, _):
            start = group_start(g, levels)
            for i in range(margin):
                where = pl.ds(start * LANES8 + first + i, LANES8, stride=LANES8)
                control, east, north, mask = (ref[where, :] for ref in refs)
                mask = mask.astype(F32)
                for f, x in enumerate((mask * control, mask, east, north)):
                    out_ref[f * margin + i, lanes_of(g), :] = x
            return 0
        lax.fori_loop(0, groups, step, 0)
    pl.when((block == 0) & (odd == 1))(lambda: edge(inner_ref, 0))
    pl.when((block == 0) & (odd == 0))(lambda: edge(outer_ref, 0))
    pl.when((block == last) & (odd == 0))(lambda: edge(inner_ref, LANES8 - margin))
    pl.when((block == last) & (odd == 1))(lambda: edge(outer_ref, LANES8 - margin))


def edge_sends(groups, margin, odd, natural):
    levels, rows, cols = natural[0].shape
    slabs, _ = slabs_of(groups)
    natural = [pltpu.with_memory_space_constraint(x, pltpu.HBM) for x in natural]
    return pl.pallas_call(functools.partial(sends_kernel, groups, levels, margin), grid=(rows // LANES8,), name="edge_sends",
        out_shape=[jax.ShapeDtypeStruct((slabs, rows, LANES8, 128), F32)] * 2 + [jax.ShapeDtypeStruct((4 * margin, LANES8 * groups, cols), F32)] * 2,
        in_specs=[pl.BlockSpec(memory_space=pltpu.SMEM)] + [pl.BlockSpec((levels, LANES8, cols), lambda i: (0, i, 0))] * 4,
        out_specs=[pl.BlockSpec((slabs, LANES8, LANES8, 128), lambda i: (0, i, 0, 0))] * 2 + [pl.BlockSpec((4 * margin, LANES8 * groups, cols), lambda i: (0, 0, 0))] * 2,
        compiler_params=params(60))(odd, *natural)


def rim_kernel(groups, margin, south_in, north_in, strip_ref):
    slabs, per = slabs_of(groups)
    for slab in range(slabs):
        for f in range(4):
            for end, ref in enumerate((south_in, north_in)):
                west, east = pack_strip(slab_load(ref, f * margin, margin, slab, per), min(per, groups - slab * per), margin, margin)
                strip_ref[f, 0, slab, end * margin:(end + 1) * margin] = west
                strip_ref[f, 1, slab, end * margin:(end + 1) * margin] = east


def strip_rims(groups, margin, south_in, north_in):
    slabs, _ = slabs_of(groups)
    return pl.pallas_call(functools.partial(rim_kernel, groups, margin),
        out_shape=jax.ShapeDtypeStruct((4, 2, slabs, 2 * margin, LANES8, 128), F32),
        in_specs=[WHOLE] * 2, out_specs=WHOLE, name="strip_rims", compiler_params=params(12))(south_in, north_in)


def faces_kernel(groups, rows, margin, mask_ref, east_ref, north_ref, south_in, north_in, e_out, n_out, mask):
    tall = rows + 2 * margin
    def step(g, _):
        put = lanes_of(g)
        mask[0:margin] = south_in[margin:2 * margin, put, :]
        mask[margin:margin + rows] = mask_ref[:, put, :]
        mask[margin + rows:tall] = north_in[margin:2 * margin, put, :]
        pieces = [(0, margin, south_in, 0), (margin + rows, margin, north_in, 0)] + [(margin + i, LANES8, None, i) for i in range(0, rows, LANES8)]
        for at, count, halo, i in pieces:
            if halo is None:
                east, north = east_ref[i:i + count, put, :], north_ref[i:i + count, put, :]
            else:
                east, north = halo[2 * margin:3 * margin, put, :], halo[3 * margin:4 * margin, put, :]
            own = mask[at:at + count]
            e_out[at:at + count, put, :] = east * own * turn(own, -1)
            n_out[at:at + count, put, :] = north * own * mask[at + 1:at + count + 1]
        return 0
    mask[tall] = jnp.zeros((LANES8, 128), F32)
    lax.fori_loop(0, groups, step, 0)


def faces(groups, rows, margin, fields, south_in, north_in):
    tall = rows + 2 * margin
    return pl.pallas_call(functools.partial(faces_kernel, groups, rows, margin),
        out_shape=[jax.ShapeDtypeStruct((tall, LANES8 * groups, 128), F32)] * 2,
        in_specs=[WHOLE] * 5, out_specs=[WHOLE] * 2, name="faces", scratch_shapes=[VMEM((tall + 1, LANES8, 128), F32)],
        compiler_params=params(12))(*fields[1:], south_in, north_in)


def sweep(source, east, north, write, low, high):
    for at in range(low, high, LANES8):
        end = min(at + LANES8, high)
        u = source(at - 1, end + 1)
        rise = north(at - 1, end) * (u[1:] - u[:-1])
        u = u[1:-1]
        run = east(at, end) * (turn(u, -1) - u)
        write(at, end, u + ((run - turn(run, 1)) + (rise[1:] - rise[:-1])))


def reader(ref, *lead):
    return lambda at, end: ref[(*lead, slice(at, end))]


def writer(ref, *lead):
    def write(at, end, value):
        ref[(*lead, slice(at, end))] = value
    return write


def all_sweeps(tall, margin, states, east, north, write):
    for k in range(margin):
        now, later = states[k % 2], states[(k + 1) % 2]
        sweep(reader(now), east, north, writer(later) if k + 1 < margin else write, k + 1, tall - 1 - k)


def strip_sweeps(rows, margin, strip_refs, faces_ref, rim):
    tall = rows + 2 * margin
    last = strip_refs[margin % 2]
    def step(slab, _):
        for side in range(2):
            states = [ref.at[side, slab] for ref in strip_refs]
            all_sweeps(tall, margin, states, reader(faces_ref, side, 0, slab), reader(faces_ref, side, 1, slab), writer(states[margin % 2]))
        for i in range(0, rows, LANES8):
            _, at = place(LANES8)
            here = slice(i + margin, i + margin + LANES8)
            rim[slab, i:i + LANES8] = jnp.where(at < margin, turn(last[1, slab, here], -margin), last[0, slab, here])
        return 0
    lax.fori_loop(0, rim.shape[0], step, 0)


def put_rim(x, g, groups, margin, rim):
    _, per = slabs_of(groups)
    slab = g // per
    lane = lax.broadcasted_iota(jnp.int32, x.shape, x.ndim - 1)
    edge = rim(slab)
    shift = 128 - margin - 4 * margin * (g - slab * per)
    edge = turn(edge, shift) if isinstance(shift, int) else pltpu.roll(edge, shift, edge.ndim - 1)
    return jnp.where((lane < margin) | (lane >= 128 - margin), edge, x)


def tiles_kernel(groups, rows, margin, u_ref, south_in, north_in, e_ref, n_ref, out_ref, state_a, state_b):
    tall = rows + 2 * margin
    def step(g, _):
        put = lanes_of(g)
        fill(state_a, put, south_in, u_ref, north_in, margin, 0)
        def write(at, end, value):
            out_ref[at - margin:end - margin, put, :] = value
        all_sweeps(tall, margin, (state_a, state_b), lambda a, b: e_ref[a:b, put, :], lambda a, b: n_ref[a:b, put, :], write)
        return 0
    lax.fori_loop(0, groups, step, 0)


def tiles(groups, rows, margin, u, south_in, north_in, e, n):
    tall = rows + 2 * margin
    size = rows * LANES8 * groups * 128
    return pl.pallas_call(functools.partial(tiles_kernel, groups, rows, margin),
        out_shape=jax.ShapeDtypeStruct((rows, LANES8 * groups, 128), F32),
        in_specs=[WHOLE] * 5, out_specs=WHOLE, name="tiles", scratch_shapes=[VMEM((tall, LANES8, 128), F32)] * 2,
        cost_estimate=pl.CostEstimate(flops=40 * size, bytes_accessed=20 * size, transcendentals=0),
        compiler_params=params(16))(u, south_in, north_in, e, n)


def fill(state, put, low, middle, high, margin, offset):
    rows = middle.shape[0]
    state[0:margin] = low[offset:offset + margin, put, :]
    state[margin:margin + rows] = middle[:, put, :]
    state[margin + rows:2 * margin + rows] = high[offset:offset + margin, put, :]


def forward_kernel(rows, margin, strip_ref, from_west, from_east, rims_ref, south_corners, north_corners, rim, faces_ref, strip_a, strip_b, mask):
    tall = rows + 2 * margin
    def join(slab, _):
        for side in range(2):
            mask[side, tall] = jnp.zeros((LANES8, 128), F32)
        pieces = [(0, margin, rims_ref, 0, south_corners.at[0, slab], south_corners.at[1, slab], 0),
                  (margin + rows, margin, rims_ref, margin, north_corners.at[0, slab], north_corners.at[1, slab], 0)]
        pieces += [(margin + i, LANES8, strip_ref, i, from_west.at[slab], from_east.at[slab], i) for i in range(0, rows, LANES8)]
        for at, count, own_ref, own_at, west_ref, east_ref, in_at in pieces:
            here, there, source = slice(at, at + count), slice(own_at, own_at + count), slice(in_at, in_at + count)
            for f in range(4):
                pair = complete(f, own_ref[f, 0, slab, there], own_ref[f, 1, slab, there], west_ref[source], east_ref[source], count, margin)
                for side, value in enumerate(pair):
                    if f == 0:
                        strip_a[side, slab, here] = value
                    elif f == 1:
                        mask[side, here] = value
                    else:
                        faces_ref[side, f - 2, slab, here] = value
        for at in range(0, tall, LANES8):
            here = slice(at, at + LANES8)
            for side in range(2):
                own = mask[side, here]
                faces_ref[side, 0, slab, here] = faces_ref[side, 0, slab, here] * own * turn(own, -1)
                faces_ref[side, 1, slab, here] = faces_ref[side, 1, slab, here] * own * mask[side, at + 1:at + 1 + LANES8]
        return 0
    lax.fori_loop(0, rim.shape[0], join, 0)
    strip_sweeps(rows, margin, (strip_a, strip_b), faces_ref, rim)


def forward_strips(groups, rows, margin, *args):
    tall = rows + 2 * margin
    slabs, _ = slabs_of(groups)
    return pl.pallas_call(functools.partial(forward_kernel, rows, margin),
        out_shape=[jax.ShapeDtypeStruct((slabs, rows, LANES8, 128), F32), jax.ShapeDtypeStruct((2, 2, slabs, tall, LANES8, 128), F32)],
        in_specs=[WHOLE] * 6, out_specs=[WHOLE] * 2, name="forward_strips",
        scratch_shapes=[VMEM((2, slabs, tall, LANES8, 128), F32)] * 2 + [VMEM((2, tall + 1, LANES8, 128), F32)],
        compiler_params=params(16))(*args)


def strip_own_kernel(groups, rows, adjoint_ref, strip_ref):
    slabs, per = slabs_of(groups)
    def step(i, _):
        for slab in range(slabs):
            west, east = pack_strip(slab_load(adjoint_ref, 2 * i, 2, slab, per), min(per, groups - slab * per), 2, STEPS)
            strip_ref[0, slab, pl.ds(2 * i, 2)] = west
            strip_ref[1, slab, pl.ds(2 * i, 2)] = east
        return 0
    lax.fori_loop(0, rows // 2, step, 0)


def strip_own(groups, rows, adjoint):
    slabs, _ = slabs_of(groups)
    return pl.pallas_call(functools.partial(strip_own_kernel, groups, rows), name="strip_own",
        out_shape=jax.ShapeDtypeStruct((2, slabs, rows, LANES8, 128), F32),
        in_specs=[WHOLE], out_specs=WHOLE, compiler_params=params(12))(adjoint)


def strip_adjoint_kernel(groups, rows, margin, own_ref, south_in, north_in, strip_ref, to_east, to_west):
    quarter = (rows + 2 * margin) // 4
    slabs, per = slabs_of(groups)
    for slab in range(slabs):
        for ref, at in ((south_in, 0), (north_in, margin + rows)):
            west, east = pack_strip(slab_load(ref, 0, margin, slab, per), min(per, groups - slab * per), margin, margin)
            strip_ref[0, slab, at:at + margin] = west
            strip_ref[1, slab, at:at + margin] = east
        for side in range(2):
            for at in range(0, rows, LANES8):
                strip_ref[side, slab, margin + at:margin + at + LANES8] = own_ref[side, slab, at:at + LANES8]
        for at in range(0, quarter, 2):
            here = [slice(at + q * quarter, at + q * quarter + 2) for q in range(4)]
            sends = pack_sends([(strip_ref[0, slab, s], strip_ref[1, slab, s]) for s in here], 2, margin)
            to_east[slab, at:at + 2], to_west[slab, at:at + 2] = sends


def strip_adjoint(groups, rows, margin, own, south_in, north_in):
    tall = rows + 2 * margin
    slabs, _ = slabs_of(groups)
    return pl.pallas_call(functools.partial(strip_adjoint_kernel, groups, rows, margin),
        out_shape=[jax.ShapeDtypeStruct((2, slabs, tall, LANES8, 128), F32)] + [jax.ShapeDtypeStruct((slabs, tall // 4, LANES8, 128), F32)] * 2,
        in_specs=[WHOLE] * 3, out_specs=[WHOLE] * 3, name="strip_adjoint", compiler_params=params(12))(own, south_in, north_in)


def finish_kernel(groups, levels, rows, margin, tiles_ref, strip_ref, from_west, from_east, faces_ref, u_ref, mask_ref, out_ref, strip_a, strip_b, rim):
    quarter = (rows + 2 * margin) // 4
    for slab in range(rim.shape[0]):
        for at in range(0, quarter, 2):
            for q in range(4):
                here = slice(at + q * quarter, at + q * quarter + 2)
                pair = complete(q, strip_ref[0, slab, here], strip_ref[1, slab, here], from_west[slab, at:at + 2], from_east[slab, at:at + 2], 2, margin)
                for side in range(2):
                    strip_a[side, slab, here] = pair[side]
    strip_sweeps(rows, margin, (strip_a, strip_b), faces_ref, rim)
    def step(g, _):
        put = lanes_of(g)
        start = group_start(g, levels)
        for at in range(0, rows, LANES8):
            here = slice(at, at + LANES8)
            value = put_rim(tiles_ref[here, put, :], g, groups, margin, lambda slab: rim[slab, here])
            value = u_ref[here, put, :] + mask_ref[here, put, :] * value
            for r in range(LANES8):
                out_ref[pl.ds(start * rows + at + r, LANES8, stride=rows), :] = value[r]
        return 0
    lax.fori_loop(0, groups, step, 0)


def finish(groups, levels, rows, margin, *args):
    tall = rows + 2 * margin
    slabs, _ = slabs_of(groups)
    return pl.pallas_call(functools.partial(finish_kernel, groups, levels, rows, margin),
        out_shape=jax.ShapeDtypeStruct((levels * rows, 128), F32),
        in_specs=[WHOLE] * 7, out_specs=WHOLE, name="finish",
        scratch_shapes=[VMEM((2, slabs, tall, LANES8, 128), F32)] * 2 + [VMEM((slabs, rows, LANES8, 128), F32)],
        compiler_params=params(20))(*args)


def departures_kernel(groups, levels, equivalent_ref, obs_ref, out_ref, back_ref):
    def step(p, _):
        for g in range(groups):
            start = group_start(g, levels)
            here = slice(LANES8 * g, LANES8 * (g + 1))
            gap = obs_ref[p, levels + start:levels + start + LANES8, :] * (equivalent_ref[p, here, :] - obs_ref[p, start:start + LANES8, :])
            back_ref[p, here, :] = gap
            out_ref[p, start:start + LANES8, :] = gap
        return 0
    lax.fori_loop(0, out_ref.shape[0], step, 0, unroll=2)


def departures_of(groups, levels, equivalent, obs):
    return pl.pallas_call(functools.partial(departures_kernel, groups, levels),
        out_shape=[jax.ShapeDtypeStruct((equivalent.shape[0], levels, 128), F32), jax.ShapeDtypeStruct(equivalent.shape, F32)],
        in_specs=[WHOLE] * 2, out_specs=[WHOLE] * 2, name="departures", compiler_params=params(16))(equivalent, obs)


def place_kernel(part_ref, out_ref):
    def step(p, _):
        out_ref[:, pl.ds(pl.multiple_of(p * 128, 128), 128)] = part_ref[p]
        return 0
    lax.fori_loop(0, part_ref.shape[0], step, 0, unroll=2)


def place_departures(part):
    blocks, levels, width = part.shape
    return pl.pallas_call(place_kernel, name="place_departures",
        out_shape=jax.ShapeDtypeStruct((levels, blocks * width), F32),
        in_specs=[WHOLE], out_specs=WHOLE, compiler_params=params(12))(part)


def exchange(values, share):
    blocks, levels, width = values.shape
    if share > 1:
        values = values.reshape(blocks, levels, share, -1).transpose(0, 2, 1, 3)
    values = values.reshape(blocks * share, levels, width // share)
    values = lax.all_to_all(values, ("gx", "gy"), 0, 0, tiled=True)
    if share > 1:
        values = values.reshape(blocks, share, levels, -1).transpose(0, 2, 1, 3)
    return values.reshape(blocks, levels, width)


def pass_around(axis, forth, back):
    size = lax.axis_size(axis)
    up = [(i, (i + 1) % size) for i in range(size)]
    return lax.ppermute(forth, axis, up), lax.ppermute(back, axis, [(j, i) for i, j in up])


def swap_rounds(axis, inner, outer):
    size, odd = lax.axis_size(axis), lax.axis_index(axis) % 2 == 1
    rounds = [[pair for i in range(first, size - 1, 2) for pair in ((i, i + 1), (i + 1, i))] for first in range(2)]
    inner, outer = lax.ppermute(inner, axis, rounds[0]), lax.ppermute(outer, axis, rounds[1])
    return jnp.where(odd, inner, outer), jnp.where(odd, outer, inner)


def swap_edges(axis, forth, back):
    odd = lax.axis_index(axis) % 2 == 1
    return swap_rounds(axis, jnp.where(odd, back, forth), jnp.where(odd, forth, back))


def body(
    control,
    east_coeff,
    north_coeff,
    ocean_mask,
    corner_cells,
    corner_weights,
    obs_value,
    obs_precision,
    slot_counts,
):
    levels, rows, cols = control.shape
    slots = corner_cells.shape[1]
    capacity = slots // lax.axis_size(("gx", "gy"))
    share = 128 // capacity
    margin = STEPS
    live = (slot_counts[0][:, None] > jnp.arange(capacity)[None, :]).astype(jnp.int32).reshape(1, slots)
    groups = -(-levels // 16) * 2
    natural = (control, east_coeff, north_coeff, ocean_mask)
    odd = (lax.axis_index("gy") % 2).astype(jnp.int32).reshape(1)
    to_east, to_west, inner, outer = edge_sends(groups, margin, odd, natural)
    from_west, from_east = pass_around("gx", to_east, to_west)
    south_in, north_in = swap_rounds("gy", inner, outer)
    obs = obs_blocks(obs_value, obs_precision, live)
    obs, *_ = lax.optimization_barrier((obs, to_east, to_west))
    obs = exchange(obs, share)
    *fields, strip = stage(groups, margin, natural)
    corners = jnp.stack([from_west, from_east])
    south_corners, north_corners = swap_edges("gy", corners[:, :, rows - margin:], corners[:, :, :margin])
    rims = strip_rims(groups, margin, south_in, north_in)
    e, n = faces(groups, rows, margin, fields, south_in, north_in)
    background = tiles(groups, rows, margin, fields[0], south_in, north_in, e, n)
    rim, strip_faces = forward_strips(groups, rows, margin, strip, from_west, from_east, rims, south_corners, north_corners)
    equivalent = gather(corner_cells, corner_weights, background, rim, slots, margin)
    out, back = departures_of(groups, levels, equivalent, obs)
    sent = exchange(out, share)
    adjoint = scatter(corner_cells, corner_weights, back, rows, cols)
    south_in, north_in = swap_edges("gy", adjoint[rows - margin:], adjoint[:margin])
    own = strip_own(groups, rows, adjoint)
    strip, to_east, to_west = strip_adjoint(groups, rows, margin, own, south_in, north_in)
    from_west, from_east = pass_around("gx", to_east, to_west)
    departures = place_departures(sent)
    swept = tiles(groups, rows, margin, adjoint, south_in, north_in, e, n)
    gradient = finish(groups, levels, rows, margin, swept, strip, from_west, from_east, strip_faces, fields[0], fields[1])
    return gradient.reshape(levels, rows, cols), departures


def solution(mesh):
    return jax.shard_map(
        body,
        mesh=mesh,
        in_specs=(
            P(None, "gy", "gx"),
            P(None, "gy", "gx"),
            P(None, "gy", "gx"),
            P(None, "gy", "gx"),
            P(None, ("gx", "gy")),
            P(None, ("gx", "gy")),
            P(None, ("gx", "gy")),
            P(None, ("gx", "gy")),
            P(("gx", "gy"), None),
        ),
        out_specs=(P(None, "gy", "gx"), P(None, ("gx", "gy"))),
        check_vma=False,
    )
```

```python
import functools

import jax
import jax.numpy as jnp
from jax import lax
from jax.experimental import pallas as pl
from jax.experimental.pallas import tpu as pltpu
from jax.sharding import PartitionSpec as P


F32, BF16 = jnp.float32, jnp.bfloat16
TOGETHER = 2
VMEM = pltpu.VMEM
STEPS = 4
LANES8 = 8
WHOLE = pl.BlockSpec(memory_space=pltpu.VMEM)


def split2(x):
    hi = x.astype(BF16)
    lo = (x - hi.astype(F32)).astype(BF16)
    return hi, lo


def hats(cells_ref, weights_ref, j0, n, cols):
    c = cells_ref[0:1, pl.ds(j0, n)]
    w = weights_ref[:, pl.ds(j0, n)]
    r = c // cols
    s = c - r * cols
    east, west = w[1:2] + w[3:4], w[0:1] + w[2:3]
    north, south = w[2:3] + w[3:4], w[0:1] + w[1:2]
    return r, s, east, west, north, south


def hat(index, low, high, size):
    at = lax.broadcasted_iota(jnp.int32, (size, index.shape[1]), 0) - index
    return jnp.where(at == 0, low, jnp.where(at == 1, high, 0.0))


def gather_kernel(rows, lev, cols, nb, margin, cells_ref, weights_ref, bg_ref, rim_ref, out_ref, bb, t0, t1, rr0, rr1):
    for r in range(rows):
        parts = [put_rim(bg_ref[r, 8 * g:8 * g + 8, :], g, lev // 8, margin, lambda slab: rim_ref[slab, r]) for g in range(lev // 8)]
        hi, lo = split2(jnp.concatenate(parts, 0))
        bb[r * lev:(r + 1) * lev, 0:cols] = hi
        bb[r * lev:(r + 1) * lev, cols:2 * cols] = lo
    blk = 256
    def multiply(jb, t, rr):
        r, s, east, west, north, south = hats(cells_ref, weights_ref, pl.multiple_of(jb * blk, blk), blk, cols)
        rr[...] = hat(r, south, north, rows)
        hi, lo = split2(hat(s, west, east, cols))
        left = bb[...]
        t[...] = (jnp.dot(left, jnp.concatenate([hi, hi], 0), preferred_element_type=F32)
                  + jnp.dot(left, jnp.concatenate([lo, lo], 0), preferred_element_type=F32))
    def reduce(jb, t, rr):
        acc = jnp.zeros((lev, blk), F32)
        for r in range(rows):
            acc = acc + t[r * lev:(r + 1) * lev, :] * rr[r:r + 1, :]
        out_ref[2 * jb] = acc[:, 0:128]
        out_ref[2 * jb + 1] = acc[:, 128:256]
    def step(i, _):
        multiply(2 * i, t0, rr0)
        multiply(2 * i + 1, t1, rr1)
        reduce(2 * i, t0, rr0)
        reduce(2 * i + 1, t1, rr1)
        return 0
    lax.fori_loop(0, nb // 2, step, 0)


def gather(cells, weights, bg, rim, slots, margin):
    rows, lev, cols = bg.shape
    nb = slots // 256
    return pl.pallas_call(functools.partial(gather_kernel, rows, lev, cols, nb, margin),
        out_shape=jax.ShapeDtypeStruct((2 * nb, lev, 128), F32),
        in_specs=[pl.BlockSpec(memory_space=VMEM)] * 4,
        out_specs=pl.BlockSpec(memory_space=VMEM), name="gather",
        scratch_shapes=[VMEM((rows * lev, 2 * cols), BF16), VMEM((rows * lev, 256), F32), VMEM((rows * lev, 256), F32), VMEM((rows, 256), F32), VMEM((rows, 256), F32)],
        compiler_params=params(20),
    )(cells, weights, bg, rim)


def spread_levels(x, lev):
    levels = x.shape[0]
    full = levels // 8 * 8
    parts = [x[:full]] + ([x[levels - 8:]] if levels > full else [])
    short = lev - sum(p.shape[0] for p in parts)
    return jnp.concatenate(parts + ([jnp.zeros((short, x.shape[1]), x.dtype)] if short else []), 0)


def scatter_kernel(rows, lev, cols, nb, cells_ref, weights_ref, back_ref, out_ref, x, acc):
    blk = 256
    acc[...] = jnp.zeros_like(acc)
    def prepare(jb, column):
        r, s, east, west, north, south = hats(cells_ref, weights_ref, pl.multiple_of(jb * blk, blk), blk, cols)
        hi, lo = split2(hat(s, west, east, cols))
        right = jnp.concatenate([hi, lo], 0)
        back = jnp.concatenate([spread_levels(back_ref[2 * jb], lev), spread_levels(back_ref[2 * jb + 1], lev)], 1)
        u_hi, u_lo = split2(back * south)
        v_hi, v_lo = split2(back * north)
        one = hat(r, 1.0, 0.0, rows + 1).astype(BF16)
        for q in range(rows):
            at = jnp.broadcast_to(one[q:q + 1, :], (lev, blk))
            high, low = u_hi * at, u_lo * at
            if q:
                below = jnp.broadcast_to(one[q - 1:q, :], (lev, blk))
                high, low = high + v_hi * below, low + v_lo * below
            x[q * lev:(q + 1) * lev, column:column + blk] = high
            x[q * lev:(q + 1) * lev, column + blk:column + 2 * blk] = low
        return jnp.concatenate([right, right], 1)
    def step(i, _):
        right = jnp.concatenate([prepare(TOGETHER * i + t, 512 * t) for t in range(TOGETHER)], 1)
        acc[...] += lax.dot_general(x[...], right, (((1,), (1,)), ((), ())), preferred_element_type=F32)
        return 0
    lax.fori_loop(0, nb // TOGETHER, step, 0)
    for r in range(rows):
        a = acc[r * lev:(r + 1) * lev, :]
        out_ref[r] = a[:, 0:cols] + a[:, cols:]


def scatter(cells, weights, back, rows, cols, lev):
    nb = back.shape[0] // 2
    return pl.pallas_call(functools.partial(scatter_kernel, rows, lev, cols, nb),
        out_shape=jax.ShapeDtypeStruct((rows, lev, cols), F32),
        in_specs=[pl.BlockSpec(memory_space=VMEM)] * 3,
        out_specs=pl.BlockSpec(memory_space=VMEM), name="scatter",
        scratch_shapes=[VMEM((rows * lev, 512 * TOGETHER), BF16), VMEM((rows * lev, 256), F32)],
        compiler_params=params(24),
    )(cells, weights, back)


def group_start(g, levels):
    start, last = LANES8 * g, levels - LANES8
    return min(start, last) if isinstance(g, int) else jnp.minimum(start, last)


def params(megabytes):
    return pltpu.CompilerParams(vmem_limit_bytes=megabytes * 2**20)


def lanes_of(g):
    return pl.ds(pl.multiple_of(LANES8 * g, LANES8), LANES8)


def obs_kernel(levels, value_ref, precision_ref, live_ref, out_ref):
    def step(p, _):
        here = pl.ds(pl.multiple_of(p * 128, 128), 128)
        live = live_ref[0:1, here] > 0
        out_ref[p, 0:levels, :] = value_ref[:, here]
        out_ref[p, levels:2 * levels, :] = jnp.where(live, precision_ref[:, here], 0.0)
        return 0
    lax.fori_loop(0, out_ref.shape[0], step, 0)


def obs_blocks(value, precision, live):
    levels, slots = value.shape
    return pl.pallas_call(functools.partial(obs_kernel, levels), name="obs_blocks",
        out_shape=jax.ShapeDtypeStruct((slots // 128, -(-2 * levels // LANES8) * LANES8, 128), F32),
        in_specs=[WHOLE] * 3, out_specs=WHOLE, compiler_params=params(12))(value, precision, live)


def turn(x, shift):
    shift = shift % 128
    return pltpu.roll(x, shift, x.ndim - 1) if shift else x


def place(rows):
    lane = lax.broadcasted_iota(jnp.int32, (rows, LANES8, 128), 2)
    return lane, lane % (4 * STEPS)


def slabs_of(groups):
    slabs = -(-groups // 8)
    return slabs, -(-groups // slabs)


def pack_strip(load, groups, rows, margin):
    lane, _ = place(rows)
    width = 4 * margin
    west = east = jnp.zeros((rows, LANES8, 128), F32)
    for g in range(groups):
        x = load(g)
        here = (lane >= width * g) & (lane < width * (g + 1))
        west = jnp.where(here, turn(x, width * g + margin), west)
        east = jnp.where(here, turn(x, width * g + 2 * margin), east)
    return west, east


def pack_sends(strips, rows, margin):
    _, at = place(rows)
    to_east = to_west = jnp.zeros((rows, LANES8, 128), F32)
    for f, (west, east) in enumerate(strips):
        here = (at >= margin * f) & (at < margin * (f + 1))
        to_east = jnp.where(here, turn(east, margin * f - margin), to_east)
        to_west = jnp.where(here, turn(west, margin * f - margin), to_west)
    return to_east, to_west


def complete(f, west, east, from_west, from_east, rows, margin):
    _, at = place(rows)
    west = jnp.where(at < margin, turn(from_west, -margin * f), west)
    east = jnp.where(at >= 2 * margin, turn(from_east, 2 * margin - margin * f), east)
    return west, east


def slab_load(ref, at, count, slab, per):
    return lambda g: ref[pl.ds(at, count), LANES8 * (slab * per + g):LANES8 * (slab * per + g + 1), :]


def stage_kernel(groups, levels, margin, control_ref, east_ref, north_ref, mask_ref, *outs):
    cols = control_ref.shape[2]
    refs = [ref.reshape(levels * LANES8, cols) for ref in (control_ref, east_ref, north_ref, mask_ref)]
    *field_refs, strip_ref = outs
    def step(g, _):
        start = group_start(g, levels)
        for r in range(LANES8):
            where = pl.ds(start * LANES8 + r, LANES8, stride=LANES8)
            control, east, north, mask = (ref[where, :] for ref in refs)
            mask = mask.astype(F32)
            for ref, value in zip(field_refs, (mask * control, mask, east, north)):
                ref[r, lanes_of(g), :] = value
        return 0
    lax.fori_loop(0, groups, step, 0)
    slabs, per = slabs_of(groups)
    count = 2
    def pack(i, _):
        at = count * i
        for slab in range(slabs):
            for f in range(4):
                west, east = pack_strip(slab_load(field_refs[f], at, count, slab, per), min(per, groups - slab * per), count, margin)
                strip_ref[f, 0, slab, pl.ds(at, count)] = west
                strip_ref[f, 1, slab, pl.ds(at, count)] = east
        return 0
    lax.fori_loop(0, LANES8 // count, pack, 0)


def stage(groups, margin, natural):
    levels, rows, cols = natural[0].shape
    depth = LANES8 * groups
    slabs, _ = slabs_of(groups)
    natural = [pltpu.with_memory_space_constraint(x, pltpu.HBM) for x in natural]
    return pl.pallas_call(functools.partial(stage_kernel, groups, levels, margin),
        grid=(rows // LANES8,), name="stage",
        out_shape=[jax.ShapeDtypeStruct((rows, depth, cols), F32)] * 4
        + [jax.ShapeDtypeStruct((4, 2, slabs, rows, LANES8, 128), F32)],
        in_specs=[pl.BlockSpec((levels, LANES8, cols), lambda i: (0, i, 0))] * 4,
        out_specs=[pl.BlockSpec((LANES8, depth, cols), lambda i: (i, 0, 0))] * 4
        + [pl.BlockSpec((4, 2, slabs, LANES8, LANES8, 128), lambda i: (0, 0, 0, i, 0, 0))],
        compiler_params=params(16))(*natural)


def sends_kernel(groups, levels, margin, odd_ref, control_ref, east_ref, north_ref, mask_ref, to_east, to_west, inner_ref, outer_ref):
    cols = control_ref.shape[2]
    refs = [ref.reshape(levels * LANES8, cols) for ref in (control_ref, east_ref, north_ref, mask_ref)]
    slabs, per = slabs_of(groups)
    quad = lax.broadcasted_iota(jnp.int32, (LANES8, 128), 1) // margin
    for r in range(LANES8):
        for slab in range(slabs):
            east_out = west_out = jnp.zeros((LANES8, 128), F32)
            for g in range(min(per, groups - slab * per)):
                where = pl.ds(group_start(slab * per + g, levels) * LANES8 + r, LANES8, stride=LANES8)
                control, east, north, mask = (ref[where, :] for ref in refs)
                mask = mask.astype(F32)
                for f, x in enumerate((mask * control, mask, east, north)):
                    here = quad == 4 * g + f
                    east_out = jnp.where(here, turn(x, margin * (4 * g + f + 1) - cols), east_out)
                    west_out = jnp.where(here, turn(x, margin * (4 * g + f)), west_out)
            to_east[slab, r] = east_out
            to_west[slab, r] = west_out
    block, last = pl.program_id(0), pl.num_programs(0) - 1
    odd = odd_ref[0]
    def edge(out_ref, first):
        def step(g, _):
            start = group_start(g, levels)
            for i in range(margin):
                where = pl.ds(start * LANES8 + first + i, LANES8, stride=LANES8)
                control, east, north, mask = (ref[where, :] for ref in refs)
                mask = mask.astype(F32)
                for f, x in enumerate((mask * control, mask, east, north)):
                    out_ref[f * margin + i, lanes_of(g), :] = x
            return 0
        lax.fori_loop(0, groups, step, 0)
    pl.when((block == 0) & (odd == 1))(lambda: edge(inner_ref, 0))
    pl.when((block == 0) & (odd == 0))(lambda: edge(outer_ref, 0))
    pl.when((block == last) & (odd == 0))(lambda: edge(inner_ref, LANES8 - margin))
    pl.when((block == last) & (odd == 1))(lambda: edge(outer_ref, LANES8 - margin))


def edge_sends(groups, margin, odd, natural):
    levels, rows, cols = natural[0].shape
    slabs, _ = slabs_of(groups)
    natural = [pltpu.with_memory_space_constraint(x, pltpu.HBM) for x in natural]
    return pl.pallas_call(functools.partial(sends_kernel, groups, levels, margin), grid=(rows // LANES8,), name="edge_sends",
        out_shape=[jax.ShapeDtypeStruct((slabs, rows, LANES8, 128), F32)] * 2 + [jax.ShapeDtypeStruct((4 * margin, LANES8 * groups, cols), F32)] * 2,
        in_specs=[pl.BlockSpec(memory_space=pltpu.SMEM)] + [pl.BlockSpec((levels, LANES8, cols), lambda i: (0, i, 0))] * 4,
        out_specs=[pl.BlockSpec((slabs, LANES8, LANES8, 128), lambda i: (0, i, 0, 0))] * 2 + [pl.BlockSpec((4 * margin, LANES8 * groups, cols), lambda i: (0, 0, 0))] * 2,
        compiler_params=params(60))(odd, *natural)


def rim_kernel(groups, margin, south_in, north_in, strip_ref):
    slabs, per = slabs_of(groups)
    for slab in range(slabs):
        for f in range(4):
            for end, ref in enumerate((south_in, north_in)):
                west, east = pack_strip(slab_load(ref, f * margin, margin, slab, per), min(per, groups - slab * per), margin, margin)
                strip_ref[f, 0, slab, end * margin:(end + 1) * margin] = west
                strip_ref[f, 1, slab, end * margin:(end + 1) * margin] = east


def strip_rims(groups, margin, south_in, north_in):
    slabs, _ = slabs_of(groups)
    return pl.pallas_call(functools.partial(rim_kernel, groups, margin),
        out_shape=jax.ShapeDtypeStruct((4, 2, slabs, 2 * margin, LANES8, 128), F32),
        in_specs=[WHOLE] * 2, out_specs=WHOLE, name="strip_rims", compiler_params=params(12))(south_in, north_in)


def faces_kernel(groups, rows, margin, mask_ref, east_ref, north_ref, south_in, north_in, e_out, n_out, mask):
    tall = rows + 2 * margin
    def step(g, _):
        put = lanes_of(g)
        mask[0:margin] = south_in[margin:2 * margin, put, :]
        mask[margin:margin + rows] = mask_ref[:, put, :]
        mask[margin + rows:tall] = north_in[margin:2 * margin, put, :]
        pieces = [(0, margin, south_in, 0), (margin + rows, margin, north_in, 0)] + [(margin + i, LANES8, None, i) for i in range(0, rows, LANES8)]
        for at, count, halo, i in pieces:
            if halo is None:
                east, north = east_ref[i:i + count, put, :], north_ref[i:i + count, put, :]
            else:
                east, north = halo[2 * margin:3 * margin, put, :], halo[3 * margin:4 * margin, put, :]
            own = mask[at:at + count]
            e_out[at:at + count, put, :] = east * own * turn(own, -1)
            n_out[at:at + count, put, :] = north * own * mask[at + 1:at + count + 1]
        return 0
    mask[tall] = jnp.zeros((LANES8, 128), F32)
    lax.fori_loop(0, groups, step, 0)


def faces(groups, rows, margin, fields, south_in, north_in):
    tall = rows + 2 * margin
    return pl.pallas_call(functools.partial(faces_kernel, groups, rows, margin),
        out_shape=[jax.ShapeDtypeStruct((tall, LANES8 * groups, 128), F32)] * 2,
        in_specs=[WHOLE] * 5, out_specs=[WHOLE] * 2, name="faces", scratch_shapes=[VMEM((tall + 1, LANES8, 128), F32)],
        compiler_params=params(12))(*fields[1:], south_in, north_in)


def sweep(source, east, north, write, low, high):
    for at in range(low, high, LANES8):
        end = min(at + LANES8, high)
        u = source(at - 1, end + 1)
        rise = north(at - 1, end) * (u[1:] - u[:-1])
        u = u[1:-1]
        run = east(at, end) * (turn(u, -1) - u)
        write(at, end, u + ((run - turn(run, 1)) + (rise[1:] - rise[:-1])))


def reader(ref, *lead):
    return lambda at, end: ref[(*lead, slice(at, end))]


def writer(ref, *lead):
    def write(at, end, value):
        ref[(*lead, slice(at, end))] = value
    return write


def all_sweeps(tall, margin, states, east, north, write):
    for k in range(margin):
        now, later = states[k % 2], states[(k + 1) % 2]
        sweep(reader(now), east, north, writer(later) if k + 1 < margin else write, k + 1, tall - 1 - k)


def strip_sweeps(rows, margin, strip_refs, faces_ref, rim):
    tall = rows + 2 * margin
    last = strip_refs[margin % 2]
    def step(slab, _):
        for side in range(2):
            states = [ref.at[side, slab] for ref in strip_refs]
            all_sweeps(tall, margin, states, reader(faces_ref, side, 0, slab), reader(faces_ref, side, 1, slab), writer(states[margin % 2]))
        for i in range(0, rows, LANES8):
            _, at = place(LANES8)
            here = slice(i + margin, i + margin + LANES8)
            rim[slab, i:i + LANES8] = jnp.where(at < margin, turn(last[1, slab, here], -margin), last[0, slab, here])
        return 0
    lax.fori_loop(0, rim.shape[0], step, 0)


def put_rim(x, g, groups, margin, rim):
    _, per = slabs_of(groups)
    slab = g // per
    lane = lax.broadcasted_iota(jnp.int32, x.shape, x.ndim - 1)
    edge = rim(slab)
    shift = 128 - margin - 4 * margin * (g - slab * per)
    edge = turn(edge, shift) if isinstance(shift, int) else pltpu.roll(edge, shift, edge.ndim - 1)
    return jnp.where((lane < margin) | (lane >= 128 - margin), edge, x)


def tiles_kernel(groups, rows, margin, u_ref, south_in, north_in, e_ref, n_ref, out_ref, state_a, state_b):
    tall = rows + 2 * margin
    def step(g, _):
        put = lanes_of(g)
        fill(state_a, put, south_in, u_ref, north_in, margin, 0)
        def write(at, end, value):
            out_ref[at - margin:end - margin, put, :] = value
        all_sweeps(tall, margin, (state_a, state_b), lambda a, b: e_ref[a:b, put, :], lambda a, b: n_ref[a:b, put, :], write)
        return 0
    lax.fori_loop(0, groups, step, 0)


def tiles(groups, rows, margin, u, south_in, north_in, e, n):
    tall = rows + 2 * margin
    size = rows * LANES8 * groups * 128
    return pl.pallas_call(functools.partial(tiles_kernel, groups, rows, margin),
        out_shape=jax.ShapeDtypeStruct((rows, LANES8 * groups, 128), F32),
        in_specs=[WHOLE] * 5, out_specs=WHOLE, name="tiles", scratch_shapes=[VMEM((tall, LANES8, 128), F32)] * 2,
        cost_estimate=pl.CostEstimate(flops=40 * size, bytes_accessed=20 * size, transcendentals=0),
        compiler_params=params(16))(u, south_in, north_in, e, n)


def fill(state, put, low, middle, high, margin, offset):
    rows = middle.shape[0]
    state[0:margin] = low[offset:offset + margin, put, :]
    state[margin:margin + rows] = middle[:, put, :]
    state[margin + rows:2 * margin + rows] = high[offset:offset + margin, put, :]


def forward_kernel(rows, margin, strip_ref, from_west, from_east, rims_ref, south_corners, north_corners, rim, faces_ref, strip_a, strip_b, mask):
    tall = rows + 2 * margin
    def join(slab, _):
        for side in range(2):
            mask[side, tall] = jnp.zeros((LANES8, 128), F32)
        pieces = [(0, margin, rims_ref, 0, south_corners.at[0, slab], south_corners.at[1, slab], 0),
                  (margin + rows, margin, rims_ref, margin, north_corners.at[0, slab], north_corners.at[1, slab], 0)]
        pieces += [(margin + i, LANES8, strip_ref, i, from_west.at[slab], from_east.at[slab], i) for i in range(0, rows, LANES8)]
        for at, count, own_ref, own_at, west_ref, east_ref, in_at in pieces:
            here, there, source = slice(at, at + count), slice(own_at, own_at + count), slice(in_at, in_at + count)
            for f in range(4):
                pair = complete(f, own_ref[f, 0, slab, there], own_ref[f, 1, slab, there], west_ref[source], east_ref[source], count, margin)
                for side, value in enumerate(pair):
                    if f == 0:
                        strip_a[side, slab, here] = value
                    elif f == 1:
                        mask[side, here] = value
                    else:
                        faces_ref[side, f - 2, slab, here] = value
        for at in range(0, tall, LANES8):
            here = slice(at, at + LANES8)
            for side in range(2):
                own = mask[side, here]
                faces_ref[side, 0, slab, here] = faces_ref[side, 0, slab, here] * own * turn(own, -1)
                faces_ref[side, 1, slab, here] = faces_ref[side, 1, slab, here] * own * mask[side, at + 1:at + 1 + LANES8]
        return 0
    lax.fori_loop(0, rim.shape[0], join, 0)
    strip_sweeps(rows, margin, (strip_a, strip_b), faces_ref, rim)


def forward_strips(groups, rows, margin, *args):
    tall = rows + 2 * margin
    slabs, _ = slabs_of(groups)
    return pl.pallas_call(functools.partial(forward_kernel, rows, margin),
        out_shape=[jax.ShapeDtypeStruct((slabs, rows, LANES8, 128), F32), jax.ShapeDtypeStruct((2, 2, slabs, tall, LANES8, 128), F32)],
        in_specs=[WHOLE] * 6, out_specs=[WHOLE] * 2, name="forward_strips",
        scratch_shapes=[VMEM((2, slabs, tall, LANES8, 128), F32)] * 2 + [VMEM((2, tall + 1, LANES8, 128), F32)],
        compiler_params=params(16))(*args)


def strip_own_kernel(groups, rows, adjoint_ref, strip_ref):
    slabs, per = slabs_of(groups)
    def step(i, _):
        for slab in range(slabs):
            west, east = pack_strip(slab_load(adjoint_ref, 2 * i, 2, slab, per), min(per, groups - slab * per), 2, STEPS)
            strip_ref[0, slab, pl.ds(2 * i, 2)] = west
            strip_ref[1, slab, pl.ds(2 * i, 2)] = east
        return 0
    lax.fori_loop(0, rows // 2, step, 0)


def strip_own(groups, rows, adjoint):
    slabs, _ = slabs_of(groups)
    return pl.pallas_call(functools.partial(strip_own_kernel, groups, rows), name="strip_own",
        out_shape=jax.ShapeDtypeStruct((2, slabs, rows, LANES8, 128), F32),
        in_specs=[WHOLE], out_specs=WHOLE, compiler_params=params(12))(adjoint)


def strip_adjoint_kernel(groups, rows, margin, own_ref, south_in, north_in, strip_ref, to_east, to_west):
    quarter = (rows + 2 * margin) // 4
    slabs, per = slabs_of(groups)
    for slab in range(slabs):
        for ref, at in ((south_in, 0), (north_in, margin + rows)):
            west, east = pack_strip(slab_load(ref, 0, margin, slab, per), min(per, groups - slab * per), margin, margin)
            strip_ref[0, slab, at:at + margin] = west
            strip_ref[1, slab, at:at + margin] = east
        for side in range(2):
            for at in range(0, rows, LANES8):
                strip_ref[side, slab, margin + at:margin + at + LANES8] = own_ref[side, slab, at:at + LANES8]
        for at in range(0, quarter, 2):
            here = [slice(at + q * quarter, at + q * quarter + 2) for q in range(4)]
            sends = pack_sends([(strip_ref[0, slab, s], strip_ref[1, slab, s]) for s in here], 2, margin)
            to_east[slab, at:at + 2], to_west[slab, at:at + 2] = sends


def strip_adjoint(groups, rows, margin, own, south_in, north_in):
    tall = rows + 2 * margin
    slabs, _ = slabs_of(groups)
    return pl.pallas_call(functools.partial(strip_adjoint_kernel, groups, rows, margin),
        out_shape=[jax.ShapeDtypeStruct((2, slabs, tall, LANES8, 128), F32)] + [jax.ShapeDtypeStruct((slabs, tall // 4, LANES8, 128), F32)] * 2,
        in_specs=[WHOLE] * 3, out_specs=[WHOLE] * 3, name="strip_adjoint", compiler_params=params(12))(own, south_in, north_in)


def finish_kernel(groups, levels, rows, margin, tiles_ref, strip_ref, from_west, from_east, faces_ref, u_ref, mask_ref, out_ref, strip_a, strip_b, rim, result, sems):
    quarter = (rows + 2 * margin) // 4
    for slab in range(rim.shape[0]):
        for at in range(0, quarter, 2):
            for q in range(4):
                here = slice(at + q * quarter, at + q * quarter + 2)
                pair = complete(q, strip_ref[0, slab, here], strip_ref[1, slab, here], from_west[slab, at:at + 2], from_east[slab, at:at + 2], 2, margin)
                for side in range(2):
                    strip_a[side, slab, here] = pair[side]
    strip_sweeps(rows, margin, (strip_a, strip_b), faces_ref, rim)
    def send(g):
        fresh = LANES8 * g - group_start(g, levels)
        source = result.at[g, fresh * rows:LANES8 * rows]
        return pltpu.make_async_copy(source, out_ref.at[LANES8 * g * rows:min(LANES8 * (g + 1), levels) * rows], sems.at[g])
    live = -(-levels // LANES8)
    for g in range(live):
        put = slice(LANES8 * g, LANES8 * (g + 1))
        for at in range(0, rows, LANES8):
            here = slice(at, at + LANES8)
            value = put_rim(tiles_ref[here, put, :], g, groups, margin, lambda slab: rim[slab, here])
            value = u_ref[here, put, :] + mask_ref[here, put, :] * value
            for r in range(LANES8):
                result[g, pl.ds(at + r, LANES8, stride=rows), :] = value[r]
        send(g).start()
    for g in range(live):
        send(g).wait()


def finish(groups, levels, rows, margin, *args):
    tall = rows + 2 * margin
    slabs, _ = slabs_of(groups)
    return pl.pallas_call(functools.partial(finish_kernel, groups, levels, rows, margin),
        out_shape=jax.ShapeDtypeStruct((levels * rows, 128), F32),
        in_specs=[WHOLE] * 7, out_specs=pl.BlockSpec(memory_space=pltpu.HBM), name="finish",
        scratch_shapes=[VMEM((2, slabs, tall, LANES8, 128), F32)] * 2 + [VMEM((slabs, rows, LANES8, 128), F32), VMEM((groups, LANES8 * rows, 128), F32), pltpu.SemaphoreType.DMA((groups,))],
        compiler_params=params(20))(*args)


def departures_kernel(levels, equivalent_ref, obs_ref, out_ref):
    def step(p, _):
        for g in range(-(-levels // LANES8)):
            start = group_start(g, levels)
            here = slice(LANES8 * g, LANES8 * (g + 1))
            out_ref[p, start:start + LANES8, :] = obs_ref[p, levels + start:levels + start + LANES8, :] * (equivalent_ref[p, here, :] - obs_ref[p, start:start + LANES8, :])
        return 0
    lax.fori_loop(0, out_ref.shape[0], step, 0, unroll=2)


def departures_of(levels, equivalent, obs):
    return pl.pallas_call(functools.partial(departures_kernel, levels),
        out_shape=jax.ShapeDtypeStruct((equivalent.shape[0], levels, 128), F32),
        in_specs=[WHOLE] * 2, out_specs=WHOLE, name="departures", compiler_params=params(16))(equivalent, obs)


def place_kernel(part_ref, out_ref):
    def step(p, _):
        out_ref[:, pl.ds(pl.multiple_of(p * 128, 128), 128)] = part_ref[p]
        return 0
    lax.fori_loop(0, part_ref.shape[0], step, 0, unroll=2)


def place_departures(part):
    blocks, levels, width = part.shape
    return pl.pallas_call(place_kernel, name="place_departures",
        out_shape=jax.ShapeDtypeStruct((levels, blocks * width), F32),
        in_specs=[WHOLE], out_specs=WHOLE, compiler_params=params(12))(part)


def exchange(values, share):
    blocks, levels, width = values.shape
    if share > 1:
        values = values.reshape(blocks, levels, share, -1).transpose(0, 2, 1, 3)
    values = values.reshape(blocks * share, levels, width // share)
    values = lax.all_to_all(values, ("gx", "gy"), 0, 0, tiled=True)
    if share > 1:
        values = values.reshape(blocks, share, levels, -1).transpose(0, 2, 1, 3)
    return values.reshape(blocks, levels, width)


def pass_around(axis, forth, back):
    size = lax.axis_size(axis)
    up = [(i, (i + 1) % size) for i in range(size)]
    return lax.ppermute(forth, axis, up), lax.ppermute(back, axis, [(j, i) for i, j in up])


def swap_rounds(axis, inner, outer):
    size, odd = lax.axis_size(axis), lax.axis_index(axis) % 2 == 1
    rounds = [[pair for i in range(first, size - 1, 2) for pair in ((i, i + 1), (i + 1, i))] for first in range(2)]
    inner, outer = lax.ppermute(inner, axis, rounds[0]), lax.ppermute(outer, axis, rounds[1])
    return jnp.where(odd, inner, outer), jnp.where(odd, outer, inner)


def swap_edges(axis, forth, back):
    odd = lax.axis_index(axis) % 2 == 1
    return swap_rounds(axis, jnp.where(odd, back, forth), jnp.where(odd, forth, back))


def body(
    control,
    east_coeff,
    north_coeff,
    ocean_mask,
    corner_cells,
    corner_weights,
    obs_value,
    obs_precision,
    slot_counts,
):
    levels, rows, cols = control.shape
    slots = corner_cells.shape[1]
    capacity = slots // lax.axis_size(("gx", "gy"))
    share = 128 // capacity
    margin = STEPS
    live = (slot_counts[0][:, None] > jnp.arange(capacity)[None, :]).astype(jnp.int32).reshape(1, slots)
    groups = -(-levels // 16) * 2
    natural = (control, east_coeff, north_coeff, ocean_mask)
    odd = (lax.axis_index("gy") % 2).astype(jnp.int32).reshape(1)
    to_east, to_west, inner, outer = edge_sends(groups, margin, odd, natural)
    from_west, from_east = pass_around("gx", to_east, to_west)
    south_in, north_in = swap_rounds("gy", inner, outer)
    obs = obs_blocks(obs_value, obs_precision, live)
    obs, *_ = lax.optimization_barrier((obs, to_east, to_west))
    obs = exchange(obs, share)
    *fields, strip = stage(groups, margin, natural)
    corners = jnp.stack([from_west, from_east])
    south_corners, north_corners = swap_edges("gy", corners[:, :, rows - margin:], corners[:, :, :margin])
    rims = strip_rims(groups, margin, south_in, north_in)
    e, n = faces(groups, rows, margin, fields, south_in, north_in)
    background = tiles(groups, rows, margin, fields[0], south_in, north_in, e, n)
    rim, strip_faces = forward_strips(groups, rows, margin, strip, from_west, from_east, rims, south_corners, north_corners)
    equivalent = gather(corner_cells, corner_weights, background, rim, slots, margin)
    out = departures_of(levels, equivalent, obs)
    sent = exchange(out, share)
    adjoint = scatter(corner_cells, corner_weights, out, rows, cols, LANES8 * groups)
    south_in, north_in = swap_edges("gy", adjoint[rows - margin:], adjoint[:margin])
    own = strip_own(groups, rows, adjoint)
    strip, to_east, to_west = strip_adjoint(groups, rows, margin, own, south_in, north_in)
    from_west, from_east = pass_around("gx", to_east, to_west)
    departures = place_departures(sent)
    swept = tiles(groups, rows, margin, adjoint, south_in, north_in, e, n)
    gradient = finish(groups, levels, rows, margin, swept, strip, from_west, from_east, strip_faces, fields[0], fields[1])
    return gradient.reshape(levels, rows, cols), departures


def solution(mesh):
    return jax.shard_map(
        body,
        mesh=mesh,
        in_specs=(
            P(None, "gy", "gx"),
            P(None, "gy", "gx"),
            P(None, "gy", "gx"),
            P(None, "gy", "gx"),
            P(None, ("gx", "gy")),
            P(None, ("gx", "gy")),
            P(None, ("gx", "gy")),
            P(None, ("gx", "gy")),
            P(("gx", "gy"), None),
        ),
        out_specs=(P(None, "gy", "gx"), P(None, ("gx", "gy"))),
        check_vma=False,
    )
```
